32 devices in a mesh: grp: 2 (over x), blk: 16 (over z, y, core).
Axes of the slice: x: 2, y: 2, z: 4, core: 2. Of those that a mesh axis runs over, the one named last changes fastest.
Arguments:
- e_field: float32 [3, 128, 64, 128], P(None, 'blk', 'grp'), may hold values from -6 to 6
- h_field: float32 [3, 128, 64, 128], P(None, 'blk', 'grp'), may hold values from -6 to 6
- inv_eps: float32 [128, 64, 128], P('blk', 'grp'), may hold values from 0.08 to 1
- cot_e: float32 [3, 128, 64, 128], P(None, 'blk', 'grp'), may hold values from -6 to 6
- cot_h: float32 [3, 128, 64, 128], P(None, 'blk', 'grp'), may hold values from -6 to 6
- voxel_ids: int32 [128, 64, 128], P('blk', 'grp'), may hold values from 0 to 2047
Outputs:
- e_final: float32 [3, 128, 64, 128], P(None, 'blk', 'grp')
- h_final: float32 [3, 128, 64, 128], P(None, 'blk', 'grp')
- voxel_grad: float32 [2048], P(('grp', 'blk'))
The draws below stay inside these ranges and needn't reach their ends.
All inputs are finite; a program needn't handle non-finite values.
Results may differ from the reference program's by a relative error of at most 0.0001.
Values sent between devices are 32-bit elements; how exact they have to be, the bound alone decides.
A program may use at most 64 MiB of HBM per device.

```python
import math
import jax
import jax.numpy as jnp

NY = 128
STEPS = 4
NX = 128
NZ = 64
VOX = 2048


def plant(result, stream_key, least, largest):
    longest = result.shape.index(max(result.shape))
    spots = []
    for shift in (0, 1):
        where = [jax.random.randint(jax.random.fold_in(stream_key, axis), (), 0, length) for axis, length in enumerate(result.shape)]
        where[longest] = (where[longest] + shift) % result.shape[longest]
        spots.append(tuple(where))
    return result.at[spots[0]].set(least).at[spots[1]].set(largest)


def level_of(own_key, extent, cuts, low, top_value):
    factor_of, own = 1.0, jax.random.fold_in(own_key, 6)
    for axis_at, shards_of in cuts:
        heights = jnp.exp(jax.random.uniform(jax.random.fold_in(own, axis_at), (shards_of,), jnp.float32, low / len(cuts), top_value / len(cuts)))
        factor_of = factor_of * jnp.repeat(heights, extent[axis_at] // shards_of).reshape([-1 if axis == axis_at else 1 for axis in range(len(extent))])
    return factor_of


def noise(stream_key, dims, deviation, most, shards=(), dtype=jnp.bfloat16):
    gain = level_of(stream_key, dims, shards, -0.22, 0.18) if shards else 1.0
    drawn = jax.random.normal(stream_key, dims, jnp.float32) * deviation * gain
    return jnp.minimum(jnp.maximum(drawn, -most), most).astype(dtype)


def setup_inputs(seed: int = 0) -> dict:
    key_of = jax.random.split(jax.random.key(seed), 7)
    return {
        "e_field": noise(key_of[0], (3, NX, NZ, NY), 1.0, 6.0, ((1, 16), (2, 2)), jnp.float32),
        "h_field": noise(key_of[1], (3, NX, NZ, NY), 1.0, 6.0, ((1, 16), (2, 2)), jnp.float32),
        "inv_eps": jnp.clip(jnp.exp(math.log(1.0) - 2.5257287 * jax.random.uniform(key_of[2], (NX, NZ, NY), jnp.float32) ** level_of(key_of[2], (NX, NZ, NY), ((0, 16), (1, 2)), -0.2, 0.2)), 0.08, 1.0),
        "cot_e": noise(key_of[3], (3, NX, NZ, NY), 1.0, 6.0, ((1, 16), (2, 2)), jnp.float32),
        "cot_h": noise(key_of[4], (3, NX, NZ, NY), 1.0, 6.0, ((1, 16), (2, 2)), jnp.float32),
        "voxel_ids": plant(jax.random.randint(key_of[5], (NX, NZ, NY), 0, VOX), jax.random.fold_in(key_of[5], 1), 0, VOX - 1).astype(jnp.int32),
    }


courant = 0.5


def lax_slice(v, axis, start, stop):
    index = [slice(None)] * v.ndim
    index[axis] = slice(start, stop)
    return v[tuple(index)]


def diff_fwd(v, axis):
    size = v.shape[axis]
    upper = jnp.concatenate([lax_slice(v, axis, 1, size), jnp.zeros_like(lax_slice(v, axis, 0, 1))], axis=axis)
    return upper - v


def diff_bwd(v, axis):
    size = v.shape[axis]
    lower = jnp.concatenate([jnp.zeros_like(lax_slice(v, axis, 0, 1)), lax_slice(v, axis, 0, size - 1)], axis=axis)
    return v - lower


def curl_with(v, diff):
    vx, vy, vz = v[0], v[1], v[2]
    cx = diff(vz, 2) - diff(vy, 1)
    cy = diff(vx, 1) - diff(vz, 0)
    cz = diff(vy, 0) - diff(vx, 2)
    return jnp.stack([cx, cy, cz])


def reference(e_field, h_field, inv_eps, cot_e, cot_h, voxel_ids):
    curls = []
    for step in range(STEPS):
        h_field = h_field - courant * curl_with(e_field, diff_fwd)
        curl_now = curl_with(h_field, diff_bwd)
        curls.append(curl_now)
        e_field = e_field + courant * inv_eps[None] * curl_now
    adj_e, adj_h = cot_e, cot_h
    grad = jnp.zeros(inv_eps.shape, jnp.float32)
    for step in range(STEPS - 1, -1, -1):
        adj_h = adj_h + courant * curl_with(inv_eps[None] * adj_e, diff_fwd)
        grad = grad + courant * jnp.sum(adj_e * curls[step], axis=0)
        adj_e = adj_e - courant * curl_with(adj_h, diff_bwd)
    voxel_grad = jax.ops.segment_sum(grad.reshape(-1), voxel_ids.reshape(-1).astype(jnp.int32), num_segments=VOX)
    return e_field, h_field, voxel_grad
```

```python
import jax
import jax.numpy as jnp
from jax import lax
from jax.experimental import pallas as pl
from jax.experimental.pallas import tpu as pltpu
from jax.sharding import PartitionSpec as P

STEPS = 4
COURANT = 0.5
MESH = pl.DeviceIdType.MESH
VOX_DEV = 64
UNROLL = True
LIMIT = 60 * 1024 * 1024


def make_kernel(ng, nb, nx, nz, ny):
    n = ng * nb
    steps = STEPS
    top, end = 8, 8 + nz

    def kernel(e_in, h_in, eps_in, ce_in, ch_in, ids_in, e_out, h_out, v_out,
               E, H, G, AH, AE, CURL, eps, ids, zs_dn, zl_dn, zs_up, zl_up, cl_a, cl_b, zs_h, zl_h,
               S, R, part, in_sem, as_sem, ar_sem, *link_sems):
        xd, xu, zd, zu, ca, cb, hx, hz = (link_sems[2 * j:2 * j + 2] for j in range(8))
        grp = lax.axis_index("grp")
        blk = lax.axis_index("blk")
        me = grp * nb + blk
        lane = lax.broadcasted_iota(jnp.int32, (nz, ny), 1)
        lane_h = lax.broadcasted_iota(jnp.int32, (end, ny), 1)

        loads = [
            pltpu.make_async_copy(ce_in, AE.at[0], in_sem.at[0]),
            pltpu.make_async_copy(eps_in, eps, in_sem.at[1]),
            pltpu.make_async_copy(e_in, E.at[0, :, 1:nx + 1, top:end, :], in_sem.at[2]),
            pltpu.make_async_copy(h_in, H.at[0, :, 1:nx + 1, top:end, :], in_sem.at[3]),
            pltpu.make_async_copy(ch_in, AH.at[0, :, 1:nx + 1, top:end, :], in_sem.at[4]),
            pltpu.make_async_copy(ids_in, ids, in_sem.at[5]),
        ]
        for j in (2, 3, 0, 1, 4, 5):
            loads[j].start()

        barrier = pltpu.get_barrier_semaphore()

        @pl.loop(1, n)
        def _(j):
            other = (me + j) % n
            pl.semaphore_signal(barrier, inc=1, device_id=(other // nb, other % nb), device_id_type=MESH)

        first_x, last_x = blk == 0, blk == nb - 1
        first_z, last_z = grp == 0, grp == ng - 1
        rounds = 2 * steps - 1

        @pl.when(last_x)
        def _():
            E[0:steps, 1:3, nx + 1, top:end, :] = jnp.zeros((steps, 2, nz, ny), jnp.float32)
            G[:, 1:3, nx + 1, top:end, :] = jnp.zeros((steps - 1, 2, nz, ny), jnp.float32)

        @pl.when(first_x)
        def _():
            H[:, 1:3, 0, top:end, :] = jnp.zeros((steps + 1, 2, nz, ny), jnp.float32)
            AH[:, 1:3, 0, top:end, :] = jnp.zeros((steps, 2, nz, ny), jnp.float32)

        @pl.when(last_z)
        def _():
            zl_dn[...] = jnp.zeros_like(zl_dn)

        @pl.when(jnp.logical_or(last_z, first_x))
        def _():
            cl_a[...] = jnp.zeros_like(cl_a)

        @pl.when(jnp.logical_or(first_z, last_x))
        def _():
            cl_b[...] = jnp.zeros_like(cl_b)

        def remote(src, dst, sems, r, to):
            return pltpu.make_async_remote_copy(src, dst, sems[0].at[r], sems[1].at[r], device_id=to, device_id_type=MESH)

        def links(r, buf):
            yes_dn, yes_up = jnp.logical_not(first_x), jnp.logical_not(last_x)
            z_dn, z_up = jnp.logical_not(first_z), jnp.logical_not(last_z)
            both = jnp.logical_and
            return [
                (yes_dn, yes_up, remote(buf.at[1:3, 1, top:end, :], buf.at[1:3, nx + 1, top:end, :], xd, r, (grp, blk - 1))),
                (yes_up, yes_dn, remote(buf.at[:, nx, top:end, :], buf.at[:, 0, top:end, :], xu, r, (grp, blk + 1))),
                (z_dn, z_up, remote(zs_dn.at[r], zl_dn.at[r], zd, r, (grp - 1, blk))),
                (z_up, z_dn, remote(zs_up.at[r], zl_up.at[r], zu, r, (grp + 1, blk))),
                (both(z_dn, yes_up), both(z_up, yes_dn), remote(zs_dn.at[r, 0, nx - 1], cl_a.at[r], ca, r, (grp - 1, blk + 1))),
                (both(z_up, yes_dn), both(z_dn, yes_up), remote(zs_up.at[r, 2, 0], cl_b.at[r], cb, r, (grp + 1, blk - 1))),
            ]

        def start_links(r, buf, h0=None, part_of=slice(None)):
            jobs = [links(r, buf)[part_of], hlinks(r, h0) if h0 is not None else []]
            for sends, _, copy in jobs[0] + jobs[1]:
                used.append((sends, copy))
                pl.when(sends)(copy.start)

        def hlinks(r, h0):
            q = 0 if r == 0 else 1
            return [
                (jnp.logical_not(last_x), jnp.logical_not(first_x), remote(h0.at[1:3, nx, top:end, :], h0.at[1:3, 0, top:end, :], hx, q, (grp, blk + 1))),
                (jnp.logical_not(last_z), jnp.logical_not(first_z), remote(zs_h.at[q], zl_h.at[q], hz, q, (grp + 1, blk))),
            ]

        used = []

        def finish_links(r, buf, h0=None):
            jobs = links(r, buf) + (hlinks(r, h0) if h0 is not None else [])
            for _, gets, copy in jobs:
                pl.when(gets)(copy.wait_recv)
            for c in range(2):
                for i in range(nx):
                    buf[c, i + 1, end:end + 1, :] = zl_dn[r, c, i]
            buf[0, 0, end:end + 1, :] = cl_a[r]
            buf[2, nx + 1, top - 1:top, :] = cl_b[r]

            @pl.when(jnp.logical_not(first_z))
            def _():
                for c in range(3):
                    for i in range(nx):
                        buf[c, i + 1, top - 1:top, :] = zl_up[r, c, i]
                if h0 is not None:
                    for c in range(2):
                        for i in range(nx):
                            h0[c, i + 1, top - 1:top, :] = zl_h[0 if r == 0 else 1, c, i]

        def curl_f(buf, i):
            vx, vy, vz = (buf[c, i, 0:end, :] for c in range(3))

            def dy(v):
                return jnp.where(lane_h == ny - 1, 0.0, pltpu.roll(v, ny - 1, 1)) - v

            dxy, dxz = (buf[c, i + 1, 0:end, :] - v for c, v in ((1, vy), (2, vz)))
            dzx, dzy = (buf[c, i, 1:end + 1, :] - v for c, v in ((0, vx), (1, vy)))
            return dy(vz) - dzy, dzx - dxz, dxy - dy(vx)

        def curl_b(buf, i):
            vx, vy, vz = (buf[c, i, top:end, :] for c in range(3))

            def dy(v):
                return v - jnp.where(lane == 0, 0.0, pltpu.roll(v, 1, 1))

            dxy, dxz = (v - buf[c, i - 1, top:end, :] for c, v in ((1, vy), (2, vz)))
            dzx, dzy = (v - buf[c, i, top - 1:end - 1, :] for c, v in ((0, vx), (1, vy)))
            return dy(vz) - dzy, dzx - dxz, dxy - dy(vx)

        def each(first, last, body):
            def step(i, carry):
                body(i)
                return carry
            lax.fori_loop(first, last, step, 0, unroll=UNROLL)

        def f_step(src, prev, dst, sign):
            def body(i):
                cv = curl_f(src, i)
                for c in range(3):
                    dst[c, i, 0:end, :] = prev[c, i, 0:end, :] + sign * cv[c]

            @pl.when(jnp.logical_not(first_x))
            def _():
                vx, vy, vz = (src[c, 0, top:end, :] for c in range(3))

                def dy(v):
                    return jnp.where(lane == ny - 1, 0.0, pltpu.roll(v, ny - 1, 1)) - v

                cy = (src[0, 0, top + 1:end + 1, :] - vx) - (src[2, 1, top:end, :] - vz)
                cz = (src[1, 1, top:end, :] - vy) - dy(vx)
                dst[1, 0, top:end, :] = prev[1, 0, top:end, :] + sign * cy
                dst[2, 0, top:end, :] = prev[2, 0, top:end, :] + sign * cz

            each(1, nx + 1, body)

            @pl.when(first_z)
            def _():
                for c in range(2):
                    for i in range(1, nx + 1):
                        dst[c, i, top - 1:top, :] = jnp.zeros((1, ny), jnp.float32)

        def edge_rows(r, c, i, new):
            if c < 2:
                zs_dn[r, c, i - 1] = new[0:1, :]
            zs_up[r, c, i - 1] = new[nz - 1:nz, :]

        ra = steps
        loads[2].wait()
        for i in range(1, nx + 1):
            for c in range(3):
                edge_rows(0, c, i, E[0, c, i, top:end, :])
        loads[3].wait()
        for i in range(1, nx + 1):
            for c in range(2):
                zs_h[0, c, i - 1] = H[0, c, i, end - 1:end, :]
        pl.semaphore_wait(barrier, n - 1)
        start_links(0, E.at[0], H.at[0])
        loads[0].wait()
        loads[1].wait()

        def first_g(i):
            for c in range(3):
                g = eps[i - 1] * AE[0, c, i - 1]
                G[0, c, i, top:end, :] = g
                edge_rows(ra, c, i, g)

        each(1, nx + 1, first_g)
        loads[4].wait()
        for i in range(1, nx + 1):
            for c in range(2):
                zs_h[1, c, i - 1] = AH[0, c, i, end - 1:end, :]
        start_links(ra, G.at[0], AH.at[0])
        loads[5].wait()

        for k in range(steps):
            finish_links(k, E.at[k], H.at[0] if k == 0 else None)
            f_step(E.at[k], H.at[k], H.at[k + 1], -COURANT)
            if k == steps - 1:
                for i in range(nx):
                    for c in range(3):
                        h_out[c, i] = H[steps, c, i + 1, top:end, :]

            def e_body(i, k=k):
                cv = curl_b(H.at[k + 1], i)
                scale = COURANT * eps[i - 1]
                for c in range(3):
                    CURL[k, c, i - 1] = cv[c]
                    new = E[k, c, i, top:end, :] + scale * cv[c]
                    if k < steps - 1:
                        E[k + 1, c, i, top:end, :] = new
                        edge_rows(k + 1, c, i, new)
                    else:
                        e_out[c, i - 1] = new

            e_body(1)
            e_body(nx)
            if k < steps - 1:
                start_links(k + 1, E.at[k + 1], part_of=slice(0, 2))
            each(2, nx, e_body)
            if k == steps - 1:
                continue
            start_links(k + 1, E.at[k + 1], part_of=slice(2, 6))
            finish_links(ra + k, G.at[k], AH.at[0] if k == 0 else None)
            f_step(G.at[k], AH.at[k], AH.at[k + 1], COURANT)

            def a_body(i, k=k):
                cv = curl_b(AH.at[k + 1], i)
                for c in range(3):
                    new = AE[k, c, i - 1] - COURANT * cv[c]
                    AE[k + 1, c, i - 1] = new
                    if k < steps - 2:
                        g = eps[i - 1] * new
                        G[k + 1, c, i, top:end, :] = g
                        edge_rows(ra + k + 1, c, i, g)

            a_body(1)
            a_body(nx)
            if k < steps - 2:
                start_links(ra + k + 1, G.at[k + 1], part_of=slice(0, 2))
            each(2, nx, a_body)
            if k < steps - 2:
                start_links(ra + k + 1, G.at[k + 1], part_of=slice(2, 6))

        own = lax.broadcasted_iota(jnp.int32, (n, ny), 0)
        place = lax.broadcasted_iota(jnp.int32, (VOX_DEV, ny), 0)
        part[...] = jnp.zeros_like(part)

        def seg(i):
            grad = jnp.zeros((nz, ny), jnp.float32)
            for k in range(steps):
                for c in range(3):
                    grad = grad + AE[steps - 1 - k, c, i] * CURL[k, c, i]
            grad = COURANT * grad
            coarse = grad.astype(jnp.bfloat16).astype(jnp.float32)
            fine = grad - coarse
            v = ids[i]
            high, low = v // VOX_DEV, v % VOX_DEV
            lhs, rhs = [], []
            for z in range(nz):
                hit = high[z:z + 1, :] == own
                lhs.append(jnp.concatenate([
                    jnp.where(hit, coarse[z:z + 1, :], 0.0).astype(jnp.bfloat16),
                    jnp.where(hit, fine[z:z + 1, :], 0.0).astype(jnp.bfloat16)], axis=0))
                rhs.append(jnp.where(low[z:z + 1, :] == place, 1.0, 0.0).astype(jnp.bfloat16))
            part[...] += lax.dot_general(
                jnp.concatenate(lhs, axis=1), jnp.concatenate(rhs, axis=1),
                (((1,), (1,)), ((), ())), preferred_element_type=jnp.float32)

        lax.fori_loop(0, nx, lambda i, carry: (seg(i), carry)[1], 0, unroll=UNROLL)

        both = part[0:n, :] + part[n:2 * n, :]
        both = jnp.concatenate([both, jnp.zeros((n, 128 - VOX_DEV), jnp.float32)], axis=1)
        for d in range(n):
            S[d] = both[d:d + 1, :]

        for dg in range(ng):
            to_grp = (grp + dg) % ng

            def send_row(db, carry, to_grp=to_grp):
                to_blk = (blk + db) % nb
                pltpu.make_async_remote_copy(
                    S.at[to_grp * nb + to_blk], R.at[me], as_sem, ar_sem,
                    device_id=(to_grp, to_blk), device_id_type=MESH).start()
                return carry

            lax.fori_loop(0 if dg else 1, nb, send_row, 0, unroll=True)

        R[me] = S[me]
        rest = pl.ds(0, n - 1)
        pltpu.make_async_copy(R.at[rest], R.at[rest], ar_sem).wait()
        v_out[...] = jnp.sum(R[...], axis=0)[:, 0:VOX_DEV]
        pltpu.make_async_copy(S.at[rest], S.at[rest], as_sem).wait()
        for sends, copy in used:
            pl.when(sends)(copy.wait_send)

    return kernel


def write_out(e_in, h_in, v_in, e_out, h_out, v_out, sem):
    copies = [
        pltpu.make_async_copy(a.at[c], b.at[c], sem.at[3 * j + c])
        for j, (a, b) in enumerate(((e_in, e_out), (h_in, h_out))) for c in range(3)
    ] + [pltpu.make_async_copy(v_in, v_out, sem.at[6])]
    for copy in copies:
        copy.start()
    for copy in copies:
        copy.wait()


def solution(mesh):
    ng, nb = mesh.shape["grp"], mesh.shape["blk"]
    n = ng * nb

    def local(e_field, h_field, inv_eps, cot_e, cot_h, voxel_ids):
        _, nx, nz, ny = e_field.shape
        f32 = jnp.float32
        padded = (3, nx + 2, nz + 16, ny)
        plain = (3, nx, nz, ny)
        rounds = 2 * STEPS - 1
        dma = pltpu.SemaphoreType.DMA
        hbm = pl.BlockSpec(memory_space=pl.ANY)
        vmem = pl.BlockSpec(memory_space=pltpu.VMEM)
        e_new, h_new, vox = pl.pallas_call(
            make_kernel(ng, nb, nx, nz, ny),
            out_shape=(
                pltpu.VMEM(plain, f32),
                pltpu.VMEM(plain, f32),
                pltpu.VMEM((1, VOX_DEV), f32),
            ),
            in_specs=[hbm] * 6,
            out_specs=(vmem,) * 3,
            scratch_shapes=[
                pltpu.VMEM((STEPS + 1,) + padded, f32),
                pltpu.VMEM((STEPS + 1,) + padded, f32),
                pltpu.VMEM((STEPS - 1,) + padded, f32),
                pltpu.VMEM((STEPS,) + padded, f32),
                pltpu.VMEM((STEPS,) + plain, f32),
                pltpu.VMEM((STEPS,) + plain, f32),
                pltpu.VMEM(plain[1:], f32),
                pltpu.VMEM(plain[1:], jnp.int32),
                pltpu.VMEM((rounds, 2, nx, 1, ny), f32),
                pltpu.VMEM((rounds, 2, nx, 1, ny), f32),
                pltpu.VMEM((rounds, 3, nx, 1, ny), f32),
                pltpu.VMEM((rounds, 3, nx, 1, ny), f32),
                pltpu.VMEM((rounds, 1, ny), f32),
                pltpu.VMEM((rounds, 1, ny), f32),
                pltpu.VMEM((2, 2, nx, 1, ny), f32),
                pltpu.VMEM((2, 2, nx, 1, ny), f32),
                pltpu.VMEM((n, 1, 128), f32),
                pltpu.VMEM((n, 1, 128), f32),
                pltpu.VMEM((2 * n, VOX_DEV), f32),
                dma((6,)), dma, dma,
            ] + [dma((rounds,))] * 12 + [dma((2,))] * 4,
            compiler_params=pltpu.CompilerParams(
                collective_id=0, has_side_effects=True, vmem_limit_bytes=LIMIT),
        )(e_field, h_field, inv_eps, cot_e, cot_h, voxel_ids)
        e_new, h_new, vox = pl.pallas_call(
            write_out,
            out_shape=(
                jax.ShapeDtypeStruct(plain, f32),
                jax.ShapeDtypeStruct(plain, f32),
                jax.ShapeDtypeStruct((1, VOX_DEV), f32),
            ),
            in_specs=[hbm, hbm, hbm],
            out_specs=(hbm, hbm, hbm),
            scratch_shapes=[dma((7,))],
            compiler_params=pltpu.CompilerParams(vmem_limit_bytes=1024 * 1024),
        )(e_new, h_new, vox)
        return e_new, h_new, vox.reshape(VOX_DEV)

    field, cell = P(None, "blk", "grp", None), P("blk", "grp", None)
    return jax.shard_map(
        local, mesh=mesh,
        in_specs=(field, field, cell, field, field, cell),
        out_specs=(field, field, P(("grp", "blk"))),
        check_vma=False,
    )
```

```python
import jax
import jax.numpy as jnp
from jax import lax
from jax.experimental import pallas as pl
from jax.experimental.pallas import tpu as pltpu
from jax.sharding import PartitionSpec as P

STEPS = 4
COURANT = 0.5
MESH = pl.DeviceIdType.MESH
VOX_DEV = 64
UNROLL = True
LIMIT = 60 * 1024 * 1024


def make_kernel(ng, nb, nx, nz, ny):
    n = ng * nb
    steps = STEPS
    top, end = 8, 8 + nz
    pad, deep = 16, 16 + nz
    lo, hi = pad - 8, deep + 8
    first, past, spare = 2, nx + 2, nx + 4
    z_up = [("e", c, deep - 1, pad - 1) for c in range(3)] + [("e", c, deep - 2, pad - 2) for c in range(3)]
    z_up += [("h", c, deep - 2, pad - 2) for c in range(2)] + [("h", c, deep - 1, pad - 1) for c in range(3)]
    z_up += [("p", 0, deep - 1, pad - 1)]
    z_dn = [("e", c, pad, deep) for c in range(3)] + [("e", c, pad + 1, deep + 1) for c in range(2)]
    z_dn += [("h", c, pad, deep) for c in range(3)] + [("p", 0, pad, deep)]
    near, far = (past - 1, first - 1), (first, past)
    corners = [
        (1, -1, [("e", c, *far, deep - 1, pad - 1) for c in range(3)]
         + [("e", 2, first + 1, past + 1, deep - 1, pad - 1), ("e", 2, *far, deep - 2, pad - 2)]
         + [("h", c, *far, deep - 1, pad - 1) for c in range(2)] + [("p", 0, *far, deep - 1, pad - 1)]),
        (1, 1, [(a, c, *near, deep - 1, pad - 1) for a in ("e", "h") for c in range(3)]),
        (-1, 1, [("e", c, *near, pad, deep) for c in range(3)]
         + [("e", 0, *near, pad + 1, deep + 1), ("e", 0, past - 2, first - 2, pad, deep)]
         + [("h", c, *near, pad, deep) for c in (1, 2)] + [("p", 0, *near, pad, deep)]),
        (-1, -1, [("e", c, *far, pad, deep) for c in range(3)]),
    ]

    def kernel(e_in, h_in, eps_in, ce_in, ch_in, ids_in, e_out, h_out, v_out,
               E, H, EP, fq, fqr, qa, qr, zus, zur, zds, zdr, cs, cr,
               G, AH, AE, CURL, eps, ids, zs_dn, zl_dn, zs_up, zl_up, cl_a, cl_b, zs_h, zl_h,
               S, R, part, in_sem, as_sem, ar_sem, fs_sem, fr_sem, *link_sems):
        xd, xu, zd, zu, ca, cb, hz = (link_sems[2 * j:2 * j + 2] for j in range(7))
        grp = lax.axis_index("grp")
        blk = lax.axis_index("blk")
        me = grp * nb + blk
        lane = lax.broadcasted_iota(jnp.int32, (nz, ny), 1)
        lane_h = lax.broadcasted_iota(jnp.int32, (end, ny), 1)
        row = lax.broadcasted_iota(jnp.int32, (nz, ny), 0)
        lane_d = lax.broadcasted_iota(jnp.int32, (hi - lo, ny), 1)

        own_x, own_z = slice(first, past), slice(pad, deep)
        loads = [
            pltpu.make_async_copy(ce_in, AE.at[0], in_sem.at[0]),
            pltpu.make_async_copy(eps_in, eps, in_sem.at[1]),
            pltpu.make_async_copy(e_in, E.at[0, :, own_x, own_z, :], in_sem.at[2]),
            pltpu.make_async_copy(h_in, H.at[0, :, own_x, own_z, :], in_sem.at[3]),
            pltpu.make_async_copy(ch_in, AH.at[0, :, 1:nx + 1, top:end, :], in_sem.at[4]),
            pltpu.make_async_copy(ids_in, ids, in_sem.at[5]),
            pltpu.make_async_copy(eps_in, EP.at[own_x, own_z, :], in_sem.at[6]),
        ]
        for j in (0, 1, 4, 2, 3, 6, 5):
            loads[j].start()

        barrier = pltpu.get_barrier_semaphore()

        @pl.loop(1, n)
        def _(j):
            other = (me + j) % n
            pl.semaphore_signal(barrier, inc=1, device_id=(other // nb, other % nb), device_id_type=MESH)

        first_x, last_x = blk == 0, blk == nb - 1
        first_z, last_z = grp == 0, grp == ng - 1
        not_first_x, not_last_x = jnp.logical_not(first_x), jnp.logical_not(last_x)
        not_first_z, not_last_z = jnp.logical_not(first_z), jnp.logical_not(last_z)
        both = jnp.logical_and

        @pl.when(last_x)
        def _():
            for k in (0, 2):
                E[k, :, past, lo:hi, :] = jnp.zeros((3, hi - lo, ny), jnp.float32)
            G[:, 1:3, nx + 1, top:end, :] = jnp.zeros((steps - 1, 2, nz, ny), jnp.float32)

        @pl.when(first_x)
        def _():
            AH[:, 1:3, 0, top:end, :] = jnp.zeros((steps, 2, nz, ny), jnp.float32)

        @pl.when(last_z)
        def _():
            for k in (0, 2):
                E[k, :, 0:nx + 4, deep:hi, :] = jnp.zeros((3, nx + 4, hi - deep, ny), jnp.float32)
            zl_dn[...] = jnp.zeros_like(zl_dn)

        @pl.when(jnp.logical_or(last_z, first_x))
        def _():
            cl_a[...] = jnp.zeros_like(cl_a)

        @pl.when(jnp.logical_or(first_z, last_x))
        def _():
            cl_b[...] = jnp.zeros_like(cl_b)

        used = []

        def each(start, stop, body):
            def step(i, carry):
                body(i)
                return carry
            lax.fori_loop(start, stop, step, 0, unroll=UNROLL)

        def part_of(name, k):
            return {"e": lambda c: E.at[k, c], "h": lambda c: H.at[k, c], "p": lambda c: EP}[name]

        def deep_send(src, dst, r, slot, to):
            return pltpu.make_async_remote_copy(
                src, dst, fs_sem.at[r, slot], fr_sem.at[r, slot], device_id=to, device_id_type=MESH)

        def x_links(r):
            k = 2 * r
            up, dn = (grp, blk + 1), (grp, blk - 1)

            def layer(buf, c, i):
                return buf.at[k, c, i, own_z, :]

            every, yz = slice(0, 3), slice(1, 3)
            ups = [
                deep_send(fq.at[r], fqr.at[r], r, 0, up),
                deep_send(layer(E, every, past - 1), layer(E, every, 1), r, 1, up),
                deep_send(layer(H, every, past - 1), layer(H, every, 1), r, 2, up),
            ]
            dns = [
                deep_send(layer(E, every, first), layer(E, every, past), r, 3, dn),
                deep_send(layer(E, yz, first + 1), layer(E, yz, past + 1), r, 4, dn),
                deep_send(layer(H, every, first), layer(H, every, past), r, 5, dn),
            ]
            if r == 0:
                ups.append(deep_send(EP.at[past - 1, own_z, :], EP.at[1, own_z, :], r, 6, up))
                dns.append(deep_send(EP.at[first, own_z, :], EP.at[past, own_z, :], r, 7, dn))
            return [(not_last_x, not_first_x, copy) for copy in ups] + [(not_first_x, not_last_x, copy) for copy in dns]

        def half_curl(vx, vy, vz, vx_up):
            up_x = jnp.where(row == nz - 1, 0.0, vx_up)
            up_y = jnp.where(lane == ny - 1, 0.0, pltpu.roll(vx, ny - 1, 1))
            return up_x - vx + vz, -vy - (up_y - vx)

        def forward_half(r):
            k, i = 2 * r, past - 2
            vx, vy, vz = (E[k, c, i, own_z, :] for c in range(3))
            cy, cz = half_curl(vx, vy, vz, E[k, 0, i, pad + 1:deep + 1, :])
            fq[r, 0] = H[k, 1, i, own_z, :] - COURANT * cy
            fq[r, 1] = H[k, 2, i, own_z, :] - COURANT * cz

        def adjoint_half(k):
            vx, vy, vz = (G[k, c, nx, top:end, :] for c in range(3))
            cy, cz = half_curl(vx, vy, vz, G[k, 0, nx, top + 1:end + 1, :])
            qa[k, 0] = AH[k, 1, nx, top:end, :] + COURANT * cy
            qa[k, 1] = AH[k, 2, nx, top:end, :] + COURANT * cz

        def z_links(r):
            nu, nd = (12, 9) if r == 0 else (11, 8)
            jobs = [
                (not_last_z, not_first_z, deep_send(zus.at[r, 0:nu], zur.at[r, 0:nu], r, 8, (grp + 1, blk))),
                (not_first_z, not_last_z, deep_send(zds.at[r, 0:nd], zdr.at[r, 0:nd], r, 9, (grp - 1, blk))),
            ]
            has = {1: (not_last_z, not_first_z), -1: (not_first_z, not_last_z)}
            has_x = {1: (not_last_x, not_first_x), -1: (not_first_x, not_last_x)}
            for j, (dg, db, _) in enumerate(corners):
                jobs.append((
                    both(has[dg][0], has_x[db][0]), both(has[dg][1], has_x[db][1]),
                    deep_send(cs.at[r, j], cr.at[r, j], r, 10 + j, (grp + dg, blk + db))))
            return jobs

        def pack(r):
            k = 2 * r
            for table, buf in ((z_up, zus), (z_dn, zds)):
                for j, (name, c, row, _) in enumerate(table):
                    if name == "p" and r:
                        continue
                    ref = part_of(name, k)(c)
                    for i in range(nx):
                        buf[r, j, i] = ref[i + first, row:row + 1, :]
            for q, (_, _, rows) in enumerate(corners):
                for j, (name, c, layer, _, row, _) in enumerate(rows):
                    if name == "p" and r:
                        continue
                    cs[r, q, j] = part_of(name, k)(c)[layer, row:row + 1, :]

        def unpack(r):
            k = 2 * r
            for table, buf, cond in ((z_up, zur, not_first_z), (z_dn, zdr, not_last_z)):
                @pl.when(cond)
                def _(table=table, buf=buf):
                    for j, (name, c, _, row) in enumerate(table):
                        if name == "p" and r:
                            continue
                        ref = part_of(name, k)(c)
                        for i in range(nx):
                            ref[i + first, row:row + 1, :] = buf[r, j, i]
            for q, (job, (_, _, rows)) in enumerate(zip(z_links(r)[2:], corners)):
                @pl.when(job[1])
                def _(q=q, rows=rows):
                    for j, (name, c, _, layer, _, row) in enumerate(rows):
                        if name == "p" and r:
                            continue
                        part_of(name, k)(c)[layer, row:row + 1, :] = cr[r, q, j]

        def start(jobs):
            for sends, _, copy in jobs:
                used.append((sends, copy))
                pl.when(sends)(copy.start)

        def finish(jobs):
            for _, gets, copy in jobs:
                pl.when(gets)(copy.wait_recv)

        def curl_up(buf, i, r0, r1):
            vx, vy, vz = (buf[c, i, r0:r1, :] for c in range(3))
            last = lane_d[0:r1 - r0] == ny - 1

            def dy(v):
                return jnp.where(last, 0.0, pltpu.roll(v, ny - 1, 1)) - v

            dxy, dxz = (buf[c, i + 1, r0:r1, :] - v for c, v in ((1, vy), (2, vz)))
            dzx, dzy = (buf[c, i, r0 + 1:r1 + 1, :] - v for c, v in ((0, vx), (1, vy)))
            return dy(vz) - dzy, dzx - dxz, dxy - dy(vx)

        def curl_dn(buf, i, r0, r1, below):
            vx, vy, vz = (buf[c, i, r0:r1, :] for c in range(3))
            head = lane_d[0:r1 - r0] == 0

            def dy(v):
                return v - jnp.where(head, 0.0, pltpu.roll(v, 1, 1))

            dxy, dxz = (v - buf[c, below, r0:r1, :] for c, v in ((1, vy), (2, vz)))
            dzx, dzy = (v - buf[c, i, r0 - 1:r1 - 1, :] for c, v in ((0, vx), (1, vy)))
            return dy(vz) - dzy, dzx - dxz, dxy - dy(vx)

        def h_step(k, i0, i1, r1):
            def body(i, to=None):
                cv = curl_up(E.at[k], i, lo, r1)
                to = i if to is None else to
                for c in range(3):
                    H[k + 1, c, to, lo:r1, :] = H[k, c, i, lo:r1, :] - COURANT * cv[c]

            lower = range(i0, first)
            if k % 2 == 0:
                r = k // 2
                H[k + 1, 1, 0, own_z, :] = fqr[r, 0] + COURANT * E[k, 2, 1, own_z, :]
                H[k + 1, 2, 0, own_z, :] = fqr[r, 1] - COURANT * E[k, 1, 1, own_z, :]
                edge = H[k + 1, 1, 0, deep - 1:deep, :] - COURANT * E[k, 0, 0, deep:deep + 1, :]
                H[k + 1, 1, 0, deep - 1:deep, :] = edge
                i0 = 1
            else:
                body(first - 1, spare)
                i0, lower = first, (spare,)
            each(i0, i1, body)

            @pl.when(first_x)
            def _():
                for i in lower:
                    H[k + 1, :, i, lo:r1, :] = jnp.zeros((3, r1 - lo, ny), jnp.float32)

            @pl.when(first_z)
            def _():
                for i in range(i0, i1):
                    H[k + 1, :, i, lo:pad, :] = jnp.zeros((3, pad - lo, ny), jnp.float32)

        def e_wide(k):
            def outer(i):
                cv = curl_dn(H.at[k + 1], i, lo, hi, i - 1)
                scale = COURANT * EP[i, lo:hi, :]
                for c in range(3):
                    E[k + 1, c, i, lo:hi, :] = E[k, c, i, lo:hi, :] + scale * cv[c]
                return cv

            def inner(i):
                cv = outer(i)
                for c in range(3):
                    CURL[k, c, i - first] = cv[c][8:8 + nz]

            outer(first - 1)
            each(first, past, inner)
            outer(past)

            @pl.when(last_x)
            def _():
                E[k + 1, :, past, lo:hi, :] = jnp.zeros((3, hi - lo, ny), jnp.float32)

            @pl.when(last_z)
            def _():
                for i in range(first - 1, past + 1):
                    E[k + 1, :, i, deep:hi, :] = jnp.zeros((3, hi - deep, ny), jnp.float32)

        def e_own(k, dst):
            def body(i, below=None):
                cv = curl_dn(H.at[k + 1], i, pad, deep, i - 1 if below is None else below)
                scale = COURANT * eps[i - first]
                for c in range(3):
                    CURL[k, c, i - first] = cv[c]
                    dst(c, i, E[k, c, i, own_z, :] + scale * cv[c])
            return body

        def remote(src, dst, sems, r, to):
            return pltpu.make_async_remote_copy(src, dst, sems[0].at[r], sems[1].at[r], device_id=to, device_id_type=MESH)

        def links(r, buf):
            return [
                (not_first_x, not_last_x, remote(buf.at[1:3, 1, top:end, :], buf.at[1:3, nx + 1, top:end, :], xd, r, (grp, blk - 1))),
                (not_last_x, not_first_x, remote(qa.at[r], qr.at[r], xu, r, (grp, blk + 1))),
                (not_first_z, not_last_z, remote(zs_dn.at[r], zl_dn.at[r], zd, r, (grp - 1, blk))),
                (not_last_z, not_first_z, remote(zs_up.at[r], zl_up.at[r], zu, r, (grp + 1, blk))),
                (both(not_first_z, not_last_x), both(not_last_z, not_first_x), remote(zs_dn.at[r, 0, nx - 1], cl_a.at[r], ca, r, (grp - 1, blk + 1))),
                (both(not_last_z, not_first_x), both(not_first_z, not_last_x), remote(zs_up.at[r, 2, 0], cl_b.at[r], cb, r, (grp + 1, blk - 1))),
            ]

        def hlinks():
            return [
                (not_last_z, not_first_z, remote(zs_h, zl_h, hz, 0, (grp + 1, blk))),
            ]

        def finish_links(r, buf, h0=None):
            finish(links(r, buf) + (hlinks() if h0 is not None else []))
            for c in range(2):
                for i in range(nx):
                    buf[c, i + 1, end:end + 1, :] = zl_dn[r, c, i]
            buf[2, nx + 1, top - 1:top, :] = cl_b[r]

            @pl.when(not_first_z)
            def _():
                for c in range(3):
                    for i in range(nx):
                        buf[c, i + 1, top - 1:top, :] = zl_up[r, c, i]
                if h0 is not None:
                    for c in range(2):
                        for i in range(nx):
                            h0[c, i + 1, top - 1:top, :] = zl_h[c, i]

        def curl_f(buf, i):
            vx, vy, vz = (buf[c, i, 0:end, :] for c in range(3))

            def dy(v):
                return jnp.where(lane_h == ny - 1, 0.0, pltpu.roll(v, ny - 1, 1)) - v

            dxy, dxz = (buf[c, i + 1, 0:end, :] - v for c, v in ((1, vy), (2, vz)))
            dzx, dzy = (buf[c, i, 1:end + 1, :] - v for c, v in ((0, vx), (1, vy)))
            return dy(vz) - dzy, dzx - dxz, dxy - dy(vx)

        def curl_b(buf, i):
            vx, vy, vz = (buf[c, i, top:end, :] for c in range(3))

            def dy(v):
                return v - jnp.where(lane == 0, 0.0, pltpu.roll(v, 1, 1))

            dxy, dxz = (v - buf[c, i - 1, top:end, :] for c, v in ((1, vy), (2, vz)))
            dzx, dzy = (v - buf[c, i, top - 1:end - 1, :] for c, v in ((0, vx), (1, vy)))
            return dy(vz) - dzy, dzx - dxz, dxy - dy(vx)

        def f_step(k, src, prev, dst, sign):
            def body(i):
                cv = curl_f(src, i)
                for c in range(3):
                    dst[c, i, 0:end, :] = prev[c, i, 0:end, :] + sign * cv[c]

            @pl.when(not_first_x)
            def _():
                dst[1, 0, top:end, :] = qr[k, 0] - sign * src[2, 1, top:end, :]
                dst[2, 0, top:end, :] = qr[k, 1] + sign * src[1, 1, top:end, :]
                dst[1, 0, end - 1:end, :] = dst[1, 0, end - 1:end, :] + sign * cl_a[k]

            each(1, nx + 1, body)

            @pl.when(first_z)
            def _():
                for c in range(2):
                    for i in range(1, nx + 1):
                        dst[c, i, top - 1:top, :] = jnp.zeros((1, ny), jnp.float32)

        def edge_rows(r, c, i, new):
            if c < 2:
                zs_dn[r, c, i - 1] = new[0:1, :]
            zs_up[r, c, i - 1] = new[nz - 1:nz, :]

        def adjoint_step(k):
            finish_links(k, G.at[k], AH.at[0] if k == 0 else None)
            f_step(k, G.at[k], AH.at[k], AH.at[k + 1], COURANT)
            more = k < steps - 2

            def a_body(i):
                cv = curl_b(AH.at[k + 1], i)
                for c in range(3):
                    new = AE[k, c, i - 1] - COURANT * cv[c]
                    AE[k + 1, c, i - 1] = new
                    if more:
                        g = eps[i - 1] * new
                        G[k + 1, c, i, top:end, :] = g
                        edge_rows(k + 1, c, i, g)

            a_body(1)
            a_body(nx)
            if more:
                adjoint_half(k + 1)
                start(links(k + 1, G.at[k + 1])[0:2])
            each(2, nx, a_body)
            if more:
                start(links(k + 1, G.at[k + 1])[2:6])

        loads[0].wait()
        loads[1].wait()

        def first_g(i):
            for c in range(3):
                g = eps[i - 1] * AE[0, c, i - 1]
                G[0, c, i, top:end, :] = g
                edge_rows(0, c, i, g)

        each(1, nx + 1, first_g)
        loads[4].wait()
        for i in range(1, nx + 1):
            for c in range(2):
                zs_h[c, i - 1] = AH[0, c, i, end - 1:end, :]
        adjoint_half(0)
        for j in (2, 3, 6):
            loads[j].wait()
        forward_half(0)
        pack(0)
        pl.semaphore_wait(barrier, n - 1)
        start(links(0, G.at[0]) + hlinks())
        start(z_links(0) + x_links(0))
        loads[5].wait()

        adjoint_step(0)
        finish(x_links(0) + z_links(0))
        unpack(0)
        h_step(0, 0, past + 1, hi)
        e_wide(0)
        h_step(1, first - 1, past, deep)

        def to_next(c, i, new):
            E[2, c, i, own_z, :] = new

        def to_out(c, i, new):
            e_out[c, i - first] = new

        body = e_own(1, to_next)
        body(first, spare)
        for i in (first + 1, past - 2, past - 1):
            body(i)
        forward_half(1)
        start(x_links(1))
        each(first + 2, past - 2, body)
        pack(1)
        start(z_links(1))

        adjoint_step(1)
        adjoint_step(2)

        finish(x_links(1) + z_links(1))
        unpack(1)
        h_step(2, 0, past + 1, hi)
        e_wide(2)
        h_step(3, first - 1, past, deep)
        body = e_own(3, to_out)
        body(first, spare)
        each(first + 1, past, body)

        def h_body(i):
            for c in range(3):
                h_out[c, i] = H[steps, c, i + first, own_z, :]

        each(0, nx, h_body)

        own = lax.broadcasted_iota(jnp.int32, (n, ny), 0)
        place = lax.broadcasted_iota(jnp.int32, (VOX_DEV, ny), 0)
        part[...] = jnp.zeros_like(part)

        def seg(i):
            grad = jnp.zeros((nz, ny), jnp.float32)
            for k in range(steps):
                for c in range(3):
                    grad = grad + AE[steps - 1 - k, c, i] * CURL[k, c, i]
            grad = COURANT * grad
            coarse = grad.astype(jnp.bfloat16).astype(jnp.float32)
            fine = grad - coarse
            v = ids[i]
            high, low = v // VOX_DEV, v % VOX_DEV
            lhs, rhs = [], []
            for z in range(nz):
                hit = high[z:z + 1, :] == own
                lhs.append(jnp.concatenate([
                    jnp.where(hit, coarse[z:z + 1, :], 0.0).astype(jnp.bfloat16),
                    jnp.where(hit, fine[z:z + 1, :], 0.0).astype(jnp.bfloat16)], axis=0))
                rhs.append(jnp.where(low[z:z + 1, :] == place, 1.0, 0.0).astype(jnp.bfloat16))
            part[...] += lax.dot_general(
                jnp.concatenate(lhs, axis=1), jnp.concatenate(rhs, axis=1),
                (((1,), (1,)), ((), ())), preferred_element_type=jnp.float32)

        lax.fori_loop(0, nx, lambda i, carry: (seg(i), carry)[1], 0, unroll=UNROLL)

        total = part[0:n, :] + part[n:2 * n, :]
        total = jnp.concatenate([total, jnp.zeros((n, 128 - VOX_DEV), jnp.float32)], axis=1)
        for d in range(n):
            S[d] = total[d:d + 1, :]

        for dg in range(ng):
            to_grp = (grp + dg) % ng

            def send_row(db, carry, to_grp=to_grp):
                to_blk = (blk + db) % nb
                pltpu.make_async_remote_copy(
                    S.at[to_grp * nb + to_blk], R.at[me], as_sem, ar_sem,
                    device_id=(to_grp, to_blk), device_id_type=MESH).start()
                return carry

            lax.fori_loop(0 if dg else 1, nb, send_row, 0, unroll=True)

        R[me] = S[me]
        rest = pl.ds(0, n - 1)
        pltpu.make_async_copy(R.at[rest], R.at[rest], ar_sem).wait()
        v_out[...] = jnp.sum(R[...], axis=0)[:, 0:VOX_DEV]
        pltpu.make_async_copy(S.at[rest], S.at[rest], as_sem).wait()
        for sends, copy in used:
            pl.when(sends)(copy.wait_send)

    return kernel


def write_out(e_in, h_in, v_in, e_out, h_out, v_out, sem):
    copies = [
        pltpu.make_async_copy(a.at[c], b.at[c], sem.at[3 * j + c])
        for j, (a, b) in enumerate(((e_in, e_out), (h_in, h_out))) for c in range(3)
    ] + [pltpu.make_async_copy(v_in, v_out, sem.at[6])]
    for copy in copies:
        copy.start()
    for copy in copies:
        copy.wait()


def solution(mesh):
    ng, nb = mesh.shape["grp"], mesh.shape["blk"]
    n = ng * nb

    def local(e_field, h_field, inv_eps, cot_e, cot_h, voxel_ids):
        _, nx, nz, ny = e_field.shape
        f32 = jnp.float32
        padded = (3, nx + 2, nz + 16, ny)
        plain = (3, nx, nz, ny)
        deep = (3, nx + 5, nz + 40, ny)
        rounds = STEPS - 1
        dma = pltpu.SemaphoreType.DMA
        hbm = pl.BlockSpec(memory_space=pl.ANY)
        vmem = pl.BlockSpec(memory_space=pltpu.VMEM)
        e_new, h_new, vox = pl.pallas_call(
            make_kernel(ng, nb, nx, nz, ny),
            out_shape=(
                pltpu.VMEM(plain, f32),
                pltpu.VMEM(plain, f32),
                pltpu.VMEM((1, VOX_DEV), f32),
            ),
            in_specs=[hbm] * 6,
            out_specs=(vmem,) * 3,
            scratch_shapes=[
                pltpu.VMEM((STEPS,) + deep, f32),
                pltpu.VMEM((STEPS + 1,) + deep, f32),
                pltpu.VMEM(deep[1:], f32),
                pltpu.VMEM((2, 2, nz, ny), f32),
                pltpu.VMEM((2, 2, nz, ny), f32),
                pltpu.VMEM((rounds, 2, nz, ny), f32),
                pltpu.VMEM((rounds, 2, nz, ny), f32),
                pltpu.VMEM((2, 12, nx, 1, ny), f32),
                pltpu.VMEM((2, 12, nx, 1, ny), f32),
                pltpu.VMEM((2, 9, nx, 1, ny), f32),
                pltpu.VMEM((2, 9, nx, 1, ny), f32),
                pltpu.VMEM((2, 4, 8, 1, ny), f32),
                pltpu.VMEM((2, 4, 8, 1, ny), f32),
                pltpu.VMEM((rounds,) + padded, f32),
                pltpu.VMEM((STEPS,) + padded, f32),
                pltpu.VMEM((STEPS,) + plain, f32),
                pltpu.VMEM((STEPS,) + plain, f32),
                pltpu.VMEM(plain[1:], f32),
                pltpu.VMEM(plain[1:], jnp.int32),
                pltpu.VMEM((rounds, 2, nx, 1, ny), f32),
                pltpu.VMEM((rounds, 2, nx, 1, ny), f32),
                pltpu.VMEM((rounds, 3, nx, 1, ny), f32),
                pltpu.VMEM((rounds, 3, nx, 1, ny), f32),
                pltpu.VMEM((rounds, 1, ny), f32),
                pltpu.VMEM((rounds, 1, ny), f32),
                pltpu.VMEM((2, nx, 1, ny), f32),
                pltpu.VMEM((2, nx, 1, ny), f32),
                pltpu.VMEM((n, 1, 128), f32),
                pltpu.VMEM((n, 1, 128), f32),
                pltpu.VMEM((2 * n, VOX_DEV), f32),
                dma((7,)), dma, dma, dma((2, 14)), dma((2, 14)),
            ] + [dma((rounds,))] * 12 + [dma((1,))] * 2,
            compiler_params=pltpu.CompilerParams(
                collective_id=0, has_side_effects=True, vmem_limit_bytes=LIMIT),
        )(e_field, h_field, inv_eps, cot_e, cot_h, voxel_ids)
        e_new, h_new, vox = pl.pallas_call(
            write_out,
            out_shape=(
                jax.ShapeDtypeStruct(plain, f32),
                jax.ShapeDtypeStruct(plain, f32),
                jax.ShapeDtypeStruct((1, VOX_DEV), f32),
            ),
            in_specs=[hbm, hbm, hbm],
            out_specs=(hbm, hbm, hbm),
            scratch_shapes=[dma((7,))],
            compiler_params=pltpu.CompilerParams(vmem_limit_bytes=1024 * 1024),
        )(e_new, h_new, vox)
        return e_new, h_new, vox.reshape(VOX_DEV)

    field, cell = P(None, "blk", "grp", None), P("blk", "grp", None)
    return jax.shard_map(
        local, mesh=mesh,
        in_specs=(field, field, cell, field, field, cell),
        out_specs=(field, field, P(("grp", "blk"))),
        check_vma=False,
    )
```

```python
import jax
import jax.numpy as jnp
from jax import lax
from jax.experimental import pallas as pl
from jax.experimental.pallas import tpu as pltpu
from jax.sharding import PartitionSpec as P

STEPS = 4
COURANT = 0.5
MESH = pl.DeviceIdType.MESH
VOX_DEV = 64
STORED = 64
UNROLL = True
LIMIT = 60 * 1024 * 1024


def make_kernel(ng, nb, nx, nz, ny):
    n = ng * nb
    steps = STEPS
    stored = n <= STORED
    pad, deep = 16, 16 + nz
    lo, hi = pad - 8, deep + 8
    first, past, spare = 2, nx + 2, nx + 4
    z_up = [(a, c, deep - 1, pad - 1) for a in ("e", "h") for c in range(3)]
    z_up += [("e", c, deep - 2, pad - 2) for c in range(3)] + [("h", c, deep - 2, pad - 2) for c in range(2)]
    z_up += [("p", 0, deep - 1, pad - 1)]
    z_dn = [("e", c, pad, deep) for c in range(3)] + [("e", c, pad + 1, deep + 1) for c in range(2)]
    z_dn += [("h", c, pad, deep) for c in range(3)] + [("p", 0, pad, deep)]
    z_rows = {(0, 0): (12, 9), (0, 1): (11, 8), (1, 0): (11, 8), (1, 1): (6, 3)}
    near, far = (past - 1, first - 1), (first, past)
    corners = [
        (1, -1, [("e", c, *far, deep - 1, pad - 1) for c in range(3)]
         + [("e", 2, first + 1, past + 1, deep - 1, pad - 1), ("e", 2, *far, deep - 2, pad - 2)]
         + [("h", c, *far, deep - 1, pad - 1) for c in range(2)] + [("p", 0, *far, deep - 1, pad - 1)]),
        (1, 1, [(a, c, *near, deep - 1, pad - 1) for a in ("e", "h") for c in range(3)]),
        (-1, 1, [("e", c, *near, pad, deep) for c in range(3)]
         + [("e", 0, *near, pad + 1, deep + 1), ("e", 0, past - 2, first - 2, pad, deep)]
         + [("h", c, *near, pad, deep) for c in (1, 2)] + [("p", 0, *near, pad, deep)]),
        (-1, -1, [("e", c, *far, pad, deep) for c in range(3)]),
    ]

    def kernel(e_in, h_in, eps_in, ce_in, ch_in, ids_in, e_out, h_out, v_out,
               E, H, EP, pu, pur, pd, pdr, zus, zur, zds, zdr, cs, cr,
               AE, CURL, eps, ids,
               GR, low_hot, high_hot, S, R, part, in_sem, as_sem, ar_sem, fs_sem, fr_sem):
        grp = lax.axis_index("grp")
        blk = lax.axis_index("blk")
        me = grp * nb + blk
        lane = lax.broadcasted_iota(jnp.int32, (nz, ny), 1)
        row = lax.broadcasted_iota(jnp.int32, (nz, ny), 0)
        lane_d = lax.broadcasted_iota(jnp.int32, (hi - lo, ny), 1)

        own_x, own_z = slice(first, past), slice(pad, deep)
        loads = [
            pltpu.make_async_copy(ce_in, AE.at[0], in_sem.at[0]),
            pltpu.make_async_copy(eps_in, eps, in_sem.at[1]),
            pltpu.make_async_copy(e_in, E.at[0, 0, :, own_x, own_z, :], in_sem.at[2]),
            pltpu.make_async_copy(h_in, H.at[0, 0, :, own_x, own_z, :], in_sem.at[3]),
            pltpu.make_async_copy(ch_in, H.at[1, 0, :, own_x, own_z, :], in_sem.at[4]),
            pltpu.make_async_copy(ids_in, ids, in_sem.at[5]),
            pltpu.make_async_copy(eps_in, EP.at[own_x, own_z, :], in_sem.at[6]),
        ]
        for j in (2, 3, 6, 1, 0, 4, 5):
            loads[j].start()

        barrier = pltpu.get_barrier_semaphore()

        @pl.loop(1, n)
        def _(j):
            other = (me + j) % n
            pl.semaphore_signal(barrier, inc=1, device_id=(other // nb, other % nb), device_id_type=MESH)

        first_x, last_x = blk == 0, blk == nb - 1
        first_z, last_z = grp == 0, grp == ng - 1
        not_first_x, not_last_x = jnp.logical_not(first_x), jnp.logical_not(last_x)
        not_first_z, not_last_z = jnp.logical_not(first_z), jnp.logical_not(last_z)
        both = jnp.logical_and

        starts = [(q, k) for q in range(2) for k in (0, 2)]
        for q, k in starts:
            for i in (1, past, past + 1):
                E[q, k, :, i, own_z, :] = jnp.zeros((3, nz, ny), jnp.float32)
            for i in (1, past):
                H[q, k, :, i, own_z, :] = jnp.zeros((3, nz, ny), jnp.float32)
            H[q, k + 1, 1:3, 0, own_z, :] = jnp.zeros((2, nz, ny), jnp.float32)

        @pl.when(last_x)
        def _():
            for q, k in starts:
                E[q, k, :, past, lo:hi, :] = jnp.zeros((3, hi - lo, ny), jnp.float32)

        @pl.when(last_z)
        def _():
            for q, k in starts:
                E[q, k, :, 0:nx + 4, deep:hi, :] = jnp.zeros((3, nx + 4, hi - deep, ny), jnp.float32)

        used = []

        def each(start, stop, body):
            def step(i, carry):
                body(i)
                return carry
            lax.fori_loop(start, stop, step, 0, unroll=UNROLL)

        rates = (COURANT, -COURANT)
        def part_of(name, q, k):
            return {"e": lambda c: E.at[q, k, c], "h": lambda c: H.at[q, k, c], "p": lambda c: EP}[name]

        def deep_send(src, dst, q, r, slot, to):
            return pltpu.make_async_remote_copy(
                src, dst, fs_sem.at[q, r, slot], fr_sem.at[q, r, slot], device_id=to, device_id_type=MESH)

        def x_links(q, r):
            up, dn = (grp, blk + 1), (grp, blk - 1)
            rows = slice(0, 2 * nz if (q, r) == (1, 1) else 4 * nz + 8)
            ups = [deep_send(pu.at[q, r, rows], pur.at[q, r, rows], q, r, 0, up)]
            dns = [deep_send(pd.at[q, r, rows], pdr.at[q, r, rows], q, r, 1, dn)]
            if (q, r) == (0, 0):
                ups.append(deep_send(EP.at[past - 1, own_z, :], EP.at[1, own_z, :], q, r, 2, up))
                dns.append(deep_send(EP.at[first, own_z, :], EP.at[past, own_z, :], q, r, 3, dn))
            return [(not_last_x, not_first_x, copy) for copy in ups] + [(not_first_x, not_last_x, copy) for copy in dns]

        def piece(j):
            return slice(j * nz, (j + 1) * nz)

        line = slice(4 * nz, 4 * nz + 1)

        def next_z(v):
            return jnp.where(row == nz - 1, 0.0, pltpu.roll(v, nz - 1, 0))

        def last_z_of(v, edge):
            return jnp.where(row == 0, edge, pltpu.roll(v, 1, 0))

        def next_y(v):
            return jnp.where(lane == ny - 1, 0.0, pltpu.roll(v, ny - 1, 1))

        def last_y(v):
            return jnp.where(lane == 0, 0.0, pltpu.roll(v, 1, 1))

        def partials(q, r):
            k, rate, short = 2 * r, rates[q], (q, r) == (1, 1)

            def h_at(i, over):
                ex, ey, ez = (E[q, k, c, i, own_z, :] for c in range(3))
                oy, oz = (E[q, k, c, i + 1, own_z, :] for c in (1, 2)) if over else (0.0, 0.0)
                hx, hy, hz = (H[q, k, c, i, own_z, :] for c in range(3))
                hx = hx - rate * ((next_y(ez) - ez) - (next_z(ey) - ey))
                hy = hy - rate * ((next_z(ex) - ex) - (oz - ez))
                hz = hz - rate * ((oy - ey) - (next_y(ex) - ex))
                return (ex, ey, ez), (hx, hy, hz)

            def z_edges(e):
                c = jnp.where(first_z, 0.0, rate)
                return c * e[1][0:1, :], -c * e[0][0:1, :]

            e, h = h_at(past - 1, False)
            pu[q, r, piece(0)] = h[1]
            pu[q, r, piece(1)] = h[2]
            if short:
                pd[q, r, piece(0)] = E[q, k, 1, first, own_z, :]
                pd[q, r, piece(1)] = E[q, k, 2, first, own_z, :]
                return
            _, under = h_at(past - 2, True)
            edge_x, edge_y = z_edges(e)
            scale = rate * EP[past - 1, own_z, :]
            ex = e[0] + scale * ((h[2] - last_y(h[2])) - (h[1] - last_z_of(h[1], edge_y)))
            ey = e[1] + scale * ((h[0] - last_z_of(h[0], edge_x)) - (h[2] - under[2]))
            ez = e[2] + scale * ((h[1] - under[1]) - (h[0] - last_y(h[0])))
            pu[q, r, piece(2)] = h[1] - rate * ((next_z(ex) - ex) + ez)
            pu[q, r, piece(3)] = h[2] + rate * (ey + (next_y(ex) - ex))
            pu[q, r, line] = edge_y

            e, h = h_at(first, True)
            edge_x, edge_y = z_edges(e)
            scale = rate * EP[first, own_z, :]
            pd[q, r, piece(0)] = e[1]
            pd[q, r, piece(1)] = e[2]
            pd[q, r, piece(2)] = e[1] + scale * ((h[0] - last_z_of(h[0], edge_x)) - h[2])
            pd[q, r, piece(3)] = e[2] + scale * (h[1] - (h[0] - last_y(h[0])))
            pd[q, r, line] = edge_y

        def piece(j):
            return slice(j * nz, (j + 1) * nz)

        line = slice(4 * nz, 4 * nz + 1)

        def next_z(v):
            return jnp.where(row == nz - 1, 0.0, pltpu.roll(v, nz - 1, 0))

        def last_z_of(v, edge):
            return jnp.where(row == 0, edge, pltpu.roll(v, 1, 0))

        def next_y(v):
            return jnp.where(lane == ny - 1, 0.0, pltpu.roll(v, ny - 1, 1))

        def last_y(v):
            return jnp.where(lane == 0, 0.0, pltpu.roll(v, 1, 1))

        def partials(q, r):
            k, rate, short = 2 * r, rates[q], (q, r) == (1, 1)

            def h_at(i, over):
                ex, ey, ez = (E[q, k, c, i, own_z, :] for c in range(3))
                oy, oz = (E[q, k, c, i + 1, own_z, :] for c in (1, 2)) if over else (0.0, 0.0)
                hx, hy, hz = (H[q, k, c, i, own_z, :] for c in range(3))
                hx = hx - rate * ((next_y(ez) - ez) - (next_z(ey) - ey))
                hy = hy - rate * ((next_z(ex) - ex) - (oz - ez))
                hz = hz - rate * ((oy - ey) - (next_y(ex) - ex))
                return (ex, ey, ez), (hx, hy, hz)

            def z_edges(e):
                c = jnp.where(first_z, 0.0, rate)
                return c * e[1][0:1, :], -c * e[0][0:1, :]

            e, h = h_at(past - 1, False)
            pu[q, r, piece(0)] = h[1]
            pu[q, r, piece(1)] = h[2]
            if short:
                pd[q, r, piece(0)] = E[q, k, 1, first, own_z, :]
                pd[q, r, piece(1)] = E[q, k, 2, first, own_z, :]
                return
            _, under = h_at(past - 2, True)
            edge_x, edge_y = z_edges(e)
            scale = rate * EP[past - 1, own_z, :]
            ex = e[0] + scale * ((h[2] - last_y(h[2])) - (h[1] - last_z_of(h[1], edge_y)))
            ey = e[1] + scale * ((h[0] - last_z_of(h[0], edge_x)) - (h[2] - under[2]))
            ez = e[2] + scale * ((h[1] - under[1]) - (h[0] - last_y(h[0])))
            pu[q, r, piece(2)] = h[1] - rate * ((next_z(ex) - ex) + ez)
            pu[q, r, piece(3)] = h[2] + rate * (ey + (next_y(ex) - ex))
            pu[q, r, line] = edge_y

            e, h = h_at(first, True)
            edge_x, edge_y = z_edges(e)
            scale = rate * EP[first, own_z, :]
            pd[q, r, piece(0)] = e[1]
            pd[q, r, piece(1)] = e[2]
            pd[q, r, piece(2)] = e[1] + scale * ((h[0] - last_z_of(h[0], edge_x)) - h[2])
            pd[q, r, piece(3)] = e[2] + scale * (h[1] - (h[0] - last_y(h[0])))
            pd[q, r, line] = edge_y

        def adjoint_half(k):
            vx, vy, vz = (G[k, c, nx, top:end, :] for c in range(3))
            cy, cz = half_curl(vx, vy, vz, G[k, 0, nx, top + 1:end + 1, :])
            qa[k, 0] = AH[q, k, 1, nx, top:end, :] + rate * cy
            qa[k, 1] = AH[q, k, 2, nx, top:end, :] + rate * cz

        def z_links(q, r):
            nu, nd = z_rows[q, r]
            jobs = [
                (not_last_z, not_first_z, deep_send(zus.at[q, r, 0:nu], zur.at[q, r, 0:nu], q, r, 4, (grp + 1, blk))),
                (not_first_z, not_last_z, deep_send(zds.at[q, r, 0:nd], zdr.at[q, r, 0:nd], q, r, 5, (grp - 1, blk))),
            ]
            has = {1: (not_last_z, not_first_z), -1: (not_first_z, not_last_z)}
            has_x = {1: (not_last_x, not_first_x), -1: (not_first_x, not_last_x)}
            for j, (dg, db, _) in enumerate(corners):
                jobs.append((
                    both(has[dg][0], has_x[db][0]), both(has[dg][1], has_x[db][1]),
                    deep_send(cs.at[q, r, j], cr.at[q, r, j], q, r, 6 + j, (grp + dg, blk + db))))
            return jobs

        def pack(q, r):
            k = 2 * r
            for table, buf, count in zip((z_up, z_dn), (zus, zds), z_rows[q, r]):
                for j, (name, c, at, _) in enumerate(table[0:count]):
                    ref = part_of(name, q, k)(c)
                    for i in range(nx):
                        buf[q, r, j, i] = ref[i + first, at:at + 1, :]
            for m, (_, _, rows) in enumerate(corners):
                for j, (name, c, layer, _, at, _) in enumerate(rows):
                    if name != "p" or (q, r) == (0, 0):
                        cs[q, r, m, j] = part_of(name, q, k)(c)[layer, at:at + 1, :]

        def unpack(q, r):
            k = 2 * r
            for table, buf, cond, count in zip((z_up, z_dn), (zur, zdr), (not_first_z, not_last_z), z_rows[q, r]):
                @pl.when(cond)
                def _(table=table, buf=buf, count=count):
                    for j, (name, c, _, at) in enumerate(table[0:count]):
                        ref = part_of(name, q, k)(c)
                        for i in range(nx):
                            ref[i + first, at:at + 1, :] = buf[q, r, j, i]
            for m, (job, (_, _, rows)) in enumerate(zip(z_links(q, r)[2:], corners)):
                @pl.when(job[1])
                def _(m=m, rows=rows):
                    for j, (name, c, _, layer, _, at) in enumerate(rows):
                        if name != "p" or (q, r) == (0, 0):
                            part_of(name, q, k)(c)[layer, at:at + 1, :] = cr[q, r, m, j]
            unpack_x(q, r)

        def unpack_x(q, r):
            k = 2 * r
            for c in (1, 2):
                E[q, k, c, spare, lo:pad, :] = E[q, k, c, past, lo:pad, :]
                E[q, k, c, spare, own_z, :] = pdr[q, r, piece(c - 1)]
                E[q, k, c, spare, deep:hi, :] = E[q, k, c, past, deep:hi, :]

            @pl.when(last_x)
            def _():
                E[q, k, :, spare, lo:hi, :] = jnp.zeros((3, hi - lo, ny), jnp.float32)

        def start(jobs):
            for sends, _, copy in jobs:
                used.append((sends, copy))
                pl.when(sends)(copy.start)

        def finish(jobs):
            for _, gets, copy in jobs:
                pl.when(gets)(copy.wait_recv)

        def curl_up(buf, i, r0, r1, above):
            vx, vy, vz = (buf[c, i, r0:r1, :] for c in range(3))
            last = lane_d[0:r1 - r0] == ny - 1

            def dy(v):
                return jnp.where(last, 0.0, pltpu.roll(v, ny - 1, 1)) - v

            dxy, dxz = (buf[c, above, r0:r1, :] - v for c, v in ((1, vy), (2, vz)))
            dzx, dzy = (buf[c, i, r0 + 1:r1 + 1, :] - v for c, v in ((0, vx), (1, vy)))
            return dy(vz) - dzy, dzx - dxz, dxy - dy(vx)

        def curl_dn(buf, i, r0, r1, below):
            vx, vy, vz = (buf[c, i, r0:r1, :] for c in range(3))
            head = lane_d[0:r1 - r0] == 0

            def dy(v):
                return v - jnp.where(head, 0.0, pltpu.roll(v, 1, 1))

            dxy, dxz = (v - buf[c, below, r0:r1, :] for c, v in ((1, vy), (2, vz)))
            dzx, dzy = (v - buf[c, i, r0 - 1:r1 - 1, :] for c, v in ((0, vx), (1, vy)))
            return dy(vz) - dzy, dzx - dxz, dxy - dy(vx)

        def h_step(q, k, r1):
            r, rate, last = k // 2, rates[q], (q, k) == (1, 2)

            def body(i, to=None, above=None):
                cv = curl_up(E.at[q, k], i, lo, r1, i + 1 if above is None else above)
                to = i if to is None else to
                for c in range(3):
                    new = H[q, k, c, i, lo:r1, :] - rate * cv[c]
                    H[q, k + 1, c, to, lo:r1, :] = new
                    if (q, k) == (0, steps - 1) and to is i:
                        h_out[c, i - first] = new[8:8 + nz]

            wide = k % 2 == 0
            body(first - 1, None if wide else spare)
            each(first, past - 1, body)
            body(past - 1, None, spare)
            if wide:
                if not last:
                    body(past)
                edge = -rate * E[q, k, 0, 0, deep:deep + 1, :]
                H[q, k + 1, 1, 0, deep - 1:deep, :] = edge
                for c in (1, 2):
                    H[q, k + 1, c, spare, lo:pad, :] = H[q, k + 1, c, 1, lo:pad, :]
                    H[q, k + 1, c, spare, own_z, :] = H[q, k + 1, c, 1, own_z, :] + pur[q, r, piece(c - 1)]
                    if r1 > deep:
                        H[q, k + 1, c, spare, deep:r1, :] = H[q, k + 1, c, 1, deep:r1, :]
                if not last:
                    H[q, k + 1, 1, spare, pad - 1:pad, :] = H[q, k + 1, 1, spare, pad - 1:pad, :] + pur[q, r, line]
            else:
                for c in (1, 2):
                    H[q, k + 1, c, spare, own_z, :] = H[q, k + 1, c, spare, own_z, :] + pur[q, r, piece(c + 1)]

            @pl.when(first_x)
            def _():
                for i in (0, 1, spare) if wide else (spare,):
                    H[q, k + 1, :, i, lo:r1, :] = jnp.zeros((3, r1 - lo, ny), jnp.float32)

            @pl.when(first_z)
            def _():
                for i in [*range(first - 1, past + 1), spare] if wide else range(first, past):
                    H[q, k + 1, :, i, lo:pad, :] = jnp.zeros((3, pad - lo, ny), jnp.float32)

        def keep_curl(q, k, i, cv):
            term = 0.0
            for c in range(3):
                if q:
                    new = AE[k, c, i] - COURANT * cv[c]
                    if k < 2:
                        AE[k + 1, c, i] = new
                    term = term + new * CURL[2 - k, c, i] if k else term
                elif k < 2:
                    CURL[k, c, i] = cv[c]
                else:
                    term = term + AE[steps - 1 - k, c, i] * cv[c]
            if (q, k) == (1, 1):
                GR[i] = term
            elif k > 1:
                GR[i] = GR[i] + term

        def e_wide(q, k):
            r, rate = k // 2, rates[q]

            def outer(i, below=None):
                cv = curl_dn(H.at[q, k + 1], i, lo, hi, i - 1 if below is None else below)
                scale = rate * EP[i, lo:hi, :]
                for c in range(3):
                    E[q, k + 1, c, i, lo:hi, :] = E[q, k, c, i, lo:hi, :] + scale * cv[c]
                return cv

            def inner(i, below=None):
                cv = [v[8:8 + nz] for v in outer(i, below)]
                keep_curl(q, k, i - first, cv)

            outer(first - 1)
            inner(first, spare)
            each(first + 1, past, inner)
            outer(past)
            edge = rate * EP[1, deep:deep + 1, :] * pur[q, r, nz - 1:nz]
            E[q, k + 1, 0, 1, deep:deep + 1, :] = E[q, k + 1, 0, 1, deep:deep + 1, :] + edge
            ey = rate * pdr[q, r, 0:1]
            edge = pdr[q, r, line] - (ey - jnp.where(lane[0:1] == 0, 0.0, pltpu.roll(ey, 1, 1)))
            edge = rate * EP[past, pad - 1:pad, :] * edge
            E[q, k + 1, 2, past, pad - 1:pad, :] = E[q, k + 1, 2, past, pad - 1:pad, :] + edge
            for c in (1, 2):
                E[q, k + 1, c, spare, lo:pad, :] = E[q, k + 1, c, past, lo:pad, :]
                E[q, k + 1, c, spare, own_z, :] = E[q, k + 1, c, past, own_z, :] + pdr[q, r, piece(c + 1)]
                E[q, k + 1, c, spare, deep:hi, :] = E[q, k + 1, c, past, deep:hi, :]

            @pl.when(last_x)
            def _():
                for i in (past, spare):
                    E[q, k + 1, :, i, lo:hi, :] = jnp.zeros((3, hi - lo, ny), jnp.float32)

            @pl.when(last_z)
            def _():
                for i in [*range(first - 1, past + 1), spare]:
                    E[q, k + 1, :, i, deep:hi, :] = jnp.zeros((3, hi - deep, ny), jnp.float32)

        def e_own(q, k, dst):
            rate = rates[q]

            def body(i, below=None):
                cv = curl_dn(H.at[q, k + 1], i, pad, deep, i - 1 if below is None else below)
                scale = rate * eps[i - first]
                keep_curl(q, k, i - first, cv)
                for c in range(3):
                    dst(c, i, E[q, k, c, i, own_z, :] + scale * cv[c])
            return body

        def adjoint_last():
            def body(i, below=None):
                keep_curl(1, 2, i - first, curl_dn(H.at[1, 3], i, pad, deep, i - 1 if below is None else below))

            body(first, spare)
            each(first + 1, past, body)

        def first_g(i):
            for c in range(3):
                E[1, 0, c, i, own_z, :] = eps[i - first] * AE[0, c, i - first]

        for j in (2, 3, 6):
            loads[j].wait()
        partials(0, 0)
        pl.semaphore_wait(barrier, n - 1)
        start(x_links(0, 0))
        for j in (1, 0, 4):
            loads[j].wait()
        for i in (first, first + 1, past - 2, past - 1):
            first_g(i)
        partials(1, 0)
        start(x_links(1, 0))
        pack(0, 0)
        start(z_links(0, 0))
        each(first + 2, past - 2, first_g)
        pack(1, 0)
        start(z_links(1, 0))
        loads[5].wait()

        own = lax.broadcasted_iota(jnp.int32, (n, ny), 0)
        place = lax.broadcasted_iota(jnp.int32, (VOX_DEV, ny), 0)

        def hits(i, z):
            high = ids[i, z:z + 1, :] // VOX_DEV
            return jnp.where(high == own, 1.0, 0.0).astype(jnp.bfloat16)

        def prepare(i):
            low = ids[i] % VOX_DEV
            for z in range(nz):
                cols = slice(z * ny, (z + 1) * ny)
                low_hot[i, :, cols] = jnp.where(low[z:z + 1, :] == place, 1.0, 0.0).astype(jnp.bfloat16)
                if stored:
                    high_hot[i, :, cols] = hits(i, z)

        each(0, nx, prepare)

        def two_steps(q, r, dst, after=None):
            k = 2 * r
            finish(x_links(q, r) + z_links(q, r))
            unpack(q, r)
            h_step(q, k, hi)
            e_wide(q, k)
            h_step(q, k + 1, deep)
            body = e_own(q, k + 1, dst)
            body(first, spare)
            if r:
                each(first + 1, past, body)
                return
            for i in (first + 1, past - 2, past - 1):
                body(i)
            partials(q, 1)
            start(x_links(q, 1))
            each(first + 2, past - 2, body)
            pack(q, 1)
            start(z_links(q, 1))

        def to_next(q):
            def put(c, i, new):
                E[q, 2, c, i, own_z, :] = new
            return put

        def to_out(c, i, new):
            e_out[c, i - first] = new

        two_steps(0, 0, to_next(0))
        two_steps(1, 0, to_next(1))
        two_steps(0, 1, to_out)
        finish(x_links(1, 1) + z_links(1, 1))
        unpack(1, 1)
        h_step(1, 2, deep)
        adjoint_last()

        part[...] = jnp.zeros_like(part)

        def seg(i):
            grad = COURANT * GR[i]
            coarse = grad.astype(jnp.bfloat16).astype(jnp.float32)
            fine = grad - coarse
            lhs = []
            for z in range(nz):
                hit = high_hot[i, :, z * ny:(z + 1) * ny] if stored else hits(i, z)
                cells = []
                for v in (coarse, fine):
                    line = jnp.broadcast_to(v[z:z + 1, :], (16, ny)).astype(jnp.bfloat16)
                    cells += [hit[q:q + 16] * line for q in range(0, n, 16)]
                lhs.append(jnp.concatenate(cells, axis=0))
            part[...] += lax.dot_general(
                jnp.concatenate(lhs, axis=1), low_hot[i],
                (((1,), (1,)), ((), ())), preferred_element_type=jnp.float32)

        each(0, nx, seg)

        total = part[0:n, :] + part[n:2 * n, :]
        total = jnp.concatenate([total, jnp.zeros((n, 128 - VOX_DEV), jnp.float32)], axis=1)
        for d in range(n):
            S[d] = total[d:d + 1, :]

        for dg in reversed(range(ng)):
            to_grp = (grp + dg) % ng

            def send_row(db, carry, to_grp=to_grp):
                to_blk = (blk + db) % nb
                pltpu.make_async_remote_copy(
                    S.at[to_grp * nb + to_blk], R.at[me], as_sem, ar_sem,
                    device_id=(to_grp, to_blk), device_id_type=MESH).start()
                return carry

            lax.fori_loop(0 if dg else 1, nb, send_row, 0, unroll=True)

        R[me] = S[me]
        rest = pl.ds(0, n - 1)
        pltpu.make_async_copy(R.at[rest], R.at[rest], ar_sem).wait()
        v_out[...] = jnp.sum(R[...], axis=0)[:, 0:VOX_DEV]
        pltpu.make_async_copy(S.at[rest], S.at[rest], as_sem).wait()
        for sends, copy in used:
            pl.when(sends)(copy.wait_send)

    return kernel


def write_out(e_in, h_in, v_in, e_out, h_out, v_out, sem):
    copies = [
        pltpu.make_async_copy(a.at[c], b.at[c], sem.at[3 * j + c])
        for j, (a, b) in enumerate(((e_in, e_out), (h_in, h_out))) for c in range(3)
    ] + [pltpu.make_async_copy(v_in, v_out, sem.at[6])]
    for copy in copies:
        copy.start()
    for copy in copies:
        copy.wait()


def solution(mesh):
    ng, nb = mesh.shape["grp"], mesh.shape["blk"]
    n = ng * nb

    def local(e_field, h_field, inv_eps, cot_e, cot_h, voxel_ids):
        _, nx, nz, ny = e_field.shape
        f32 = jnp.float32
        plain = (3, nx, nz, ny)
        deep = (3, nx + 5, nz + 40, ny)
        dma = pltpu.SemaphoreType.DMA
        hbm = pl.BlockSpec(memory_space=pl.ANY)
        vmem = pl.BlockSpec(memory_space=pltpu.VMEM)
        e_new, h_new, vox = pl.pallas_call(
            make_kernel(ng, nb, nx, nz, ny),
            out_shape=(
                pltpu.VMEM(plain, f32),
                pltpu.VMEM(plain, f32),
                pltpu.VMEM((1, VOX_DEV), f32),
            ),
            in_specs=[hbm] * 6,
            out_specs=(vmem,) * 3,
            scratch_shapes=[
                pltpu.VMEM((2, STEPS) + deep, f32),
                pltpu.VMEM((2, STEPS + 1) + deep, f32),
                pltpu.VMEM(deep[1:], f32),
                pltpu.VMEM((2, 2, 4 * nz + 8, ny), f32),
                pltpu.VMEM((2, 2, 4 * nz + 8, ny), f32),
                pltpu.VMEM((2, 2, 4 * nz + 8, ny), f32),
                pltpu.VMEM((2, 2, 4 * nz + 8, ny), f32),
                pltpu.VMEM((2, 2, 12, nx, 1, ny), f32),
                pltpu.VMEM((2, 2, 12, nx, 1, ny), f32),
                pltpu.VMEM((2, 2, 9, nx, 1, ny), f32),
                pltpu.VMEM((2, 2, 9, nx, 1, ny), f32),
                pltpu.VMEM((2, 2, 4, 8, 1, ny), f32),
                pltpu.VMEM((2, 2, 4, 8, 1, ny), f32),
                pltpu.VMEM((3,) + plain, f32),
                pltpu.VMEM((2,) + plain, f32),
                pltpu.VMEM(plain[1:], f32),
                pltpu.VMEM(plain[1:], jnp.int32),
                pltpu.VMEM(plain[1:], f32),
                pltpu.VMEM((nx, VOX_DEV, nz * ny), jnp.bfloat16),
                pltpu.VMEM((nx, n if n <= STORED else 16, nz * ny), jnp.bfloat16),
                pltpu.VMEM((n, 1, 128), f32),
                pltpu.VMEM((n, 1, 128), f32),
                pltpu.VMEM((2 * n, VOX_DEV), f32),
                dma((7,)), dma, dma, dma((2, 2, 10)), dma((2, 2, 10)),
            ],
            compiler_params=pltpu.CompilerParams(
                collective_id=0, has_side_effects=True, vmem_limit_bytes=LIMIT),
        )(e_field, h_field, inv_eps, cot_e, cot_h, voxel_ids)
        e_new, h_new, vox = pl.pallas_call(
            write_out,
            out_shape=(
                jax.ShapeDtypeStruct(plain, f32),
                jax.ShapeDtypeStruct(plain, f32),
                jax.ShapeDtypeStruct((1, VOX_DEV), f32),
            ),
            in_specs=[hbm, hbm, hbm],
            out_specs=(hbm, hbm, hbm),
            scratch_shapes=[dma((7,))],
            compiler_params=pltpu.CompilerParams(vmem_limit_bytes=1024 * 1024),
        )(e_new, h_new, vox)
        return e_new, h_new, vox.reshape(VOX_DEV)

    field, cell = P(None, "blk", "grp", None), P("blk", "grp", None)
    return jax.shard_map(
        local, mesh=mesh,
        in_specs=(field, field, cell, field, field, cell),
        out_specs=(field, field, P(("grp", "blk"))),
        check_vma=False,
    )
```

```python
import jax
import jax.numpy as jnp
from jax import lax
from jax.experimental import pallas as pl
from jax.experimental.pallas import tpu as pltpu
from jax.sharding import PartitionSpec as P

STEPS = 4
COURANT = 0.5
MESH = pl.DeviceIdType.MESH
VOX_DEV = 64
STORED = 64
REACH = 1
UNROLL = True
LIMIT = 60 * 1024 * 1024


def spread(nb):
    stages, reach = [], REACH
    while reach < nb - 1:
        stages.append(reach)
        reach *= 2
    return stages


def make_kernel(ng, nb, nx, nz, ny):
    n = ng * nb
    steps = STEPS
    stored = n <= STORED
    stages = spread(nb)
    pad, deep = 16, 16 + nz
    lo, hi = pad - 8, deep + 8
    first, past, spare = 2, nx + 2, nx + 4
    z_up = [(a, c, deep - 1, pad - 1) for a in ("e", "h") for c in range(3)]
    z_up += [("e", c, deep - 2, pad - 2) for c in range(3)] + [("h", c, deep - 2, pad - 2) for c in range(2)]
    z_up += [("p", 0, deep - 1, pad - 1)]
    z_dn = [("e", c, pad, deep) for c in range(3)] + [("e", c, pad + 1, deep + 1) for c in range(2)]
    z_dn += [("h", c, pad, deep) for c in range(3)] + [("p", 0, pad, deep)]
    z_rows = {(0, 0): (12, 9), (0, 1): (11, 8), (1, 0): (11, 8), (1, 1): (6, 3)}
    near, far = (past - 1, first - 1), (first, past)
    corners = [
        (1, -1, [("e", c, *far, deep - 1, pad - 1) for c in range(3)]
         + [("e", 2, first + 1, past + 1, deep - 1, pad - 1), ("e", 2, *far, deep - 2, pad - 2)]
         + [("h", c, *far, deep - 1, pad - 1) for c in range(2)] + [("p", 0, *far, deep - 1, pad - 1)]),
        (1, 1, [(a, c, *near, deep - 1, pad - 1) for a in ("e", "h") for c in range(3)]),
        (-1, 1, [("e", c, *near, pad, deep) for c in range(3)]
         + [("e", 0, *near, pad + 1, deep + 1), ("e", 0, past - 2, first - 2, pad, deep)]
         + [("h", c, *near, pad, deep) for c in (1, 2)] + [("p", 0, *near, pad, deep)]),
        (-1, -1, [("e", c, *far, pad, deep) for c in range(3)]),
    ]

    def kernel(e_in, h_in, eps_in, ce_in, ch_in, ids_in, e_out, h_out, v_out,
               E, H, EP, pu, pur, pd, pdr, zus, zur, zds, zdr, cs, cr,
               AE, CURL, eps, ids,
               GR, low_hot, high_hot, S, R, part, in_sem, as_sem, ar_sem, fs_sem, fr_sem, known):
        grp = lax.axis_index("grp")
        blk = lax.axis_index("blk")
        me = grp * nb + blk
        lane = lax.broadcasted_iota(jnp.int32, (nz, ny), 1)
        row = lax.broadcasted_iota(jnp.int32, (nz, ny), 0)
        lane_d = lax.broadcasted_iota(jnp.int32, (hi - lo, ny), 1)

        own_x, own_z = slice(first, past), slice(pad, deep)
        loads = [
            pltpu.make_async_copy(ce_in, AE.at[0], in_sem.at[0]),
            pltpu.make_async_copy(eps_in, eps, in_sem.at[1]),
            pltpu.make_async_copy(e_in, E.at[0, 0, :, own_x, own_z, :], in_sem.at[2]),
            pltpu.make_async_copy(h_in, H.at[0, 0, :, own_x, own_z, :], in_sem.at[3]),
            pltpu.make_async_copy(ch_in, H.at[1, 0, :, own_x, own_z, :], in_sem.at[4]),
            pltpu.make_async_copy(ids_in, ids, in_sem.at[5]),
            pltpu.make_async_copy(eps_in, EP.at[own_x, own_z, :], in_sem.at[6]),
        ]
        for j in (2, 3, 6, 1, 0, 4, 5):
            loads[j].start()

        barrier = pltpu.get_barrier_semaphore()

        for db in range(-REACH, REACH + 1):
            for dg in range(ng):
                if db or dg:
                    @pl.when(jnp.logical_and(blk + db >= 0, blk + db < nb))
                    def _(db=db, dg=dg):
                        pl.semaphore_signal(
                            barrier, inc=1, device_id=((grp + dg) % ng, blk + db), device_id_type=MESH)

        near_by = ng * (jnp.minimum(blk + REACH, nb - 1) - jnp.maximum(blk - REACH, 0) + 1) - 1

        def tell(s):
            for d in (-stages[s], stages[s]):
                @pl.when(jnp.logical_and(blk + d >= 0, blk + d < nb))
                def _(d=d):
                    pl.semaphore_signal(known.at[s], inc=1, device_id=(grp, blk + d), device_id_type=MESH)

        def hear(s):
            d = stages[s]
            pl.semaphore_wait(known.at[s], jnp.where(blk >= d, 1, 0) + jnp.where(blk + d < nb, 1, 0))

        first_x, last_x = blk == 0, blk == nb - 1
        first_z, last_z = grp == 0, grp == ng - 1
        not_first_x, not_last_x = jnp.logical_not(first_x), jnp.logical_not(last_x)
        not_first_z, not_last_z = jnp.logical_not(first_z), jnp.logical_not(last_z)
        both = jnp.logical_and

        starts = [(q, k) for q in range(2) for k in (0, 2)]
        for q, k in starts:
            for i in (1, past, past + 1):
                E[q, k, :, i, own_z, :] = jnp.zeros((3, nz, ny), jnp.float32)
            for i in (1, past):
                H[q, k, :, i, own_z, :] = jnp.zeros((3, nz, ny), jnp.float32)
            H[q, k + 1, 1:3, 0, own_z, :] = jnp.zeros((2, nz, ny), jnp.float32)

        @pl.when(last_x)
        def _():
            for q, k in starts:
                E[q, k, :, past, lo:hi, :] = jnp.zeros((3, hi - lo, ny), jnp.float32)

        @pl.when(last_z)
        def _():
            for q, k in starts:
                E[q, k, :, 0:nx + 4, deep:hi, :] = jnp.zeros((3, nx + 4, hi - deep, ny), jnp.float32)

        used = []

        def each(start, stop, body):
            def step(i, carry):
                body(i)
                return carry
            lax.fori_loop(start, stop, step, 0, unroll=UNROLL)

        rates = (COURANT, -COURANT)
        def part_of(name, q, k):
            return {"e": lambda c: E.at[q, k, c], "h": lambda c: H.at[q, k, c], "p": lambda c: EP}[name]

        def deep_send(src, dst, q, r, slot, to):
            return pltpu.make_async_remote_copy(
                src, dst, fs_sem.at[q, r, slot], fr_sem.at[q, r, slot], device_id=to, device_id_type=MESH)

        def x_links(q, r):
            up, dn = (grp, blk + 1), (grp, blk - 1)
            rows = slice(0, 2 * nz if (q, r) == (1, 1) else 4 * nz + 8)
            ups = [deep_send(pu.at[q, r, rows], pur.at[q, r, rows], q, r, 0, up)]
            dns = [deep_send(pd.at[q, r, rows], pdr.at[q, r, rows], q, r, 1, dn)]
            return [(not_last_x, not_first_x, copy) for copy in ups] + [(not_first_x, not_last_x, copy) for copy in dns]

        def eps_links():
            return [
                (not_last_x, not_first_x, deep_send(eps_in.at[nx - 1], EP.at[1, own_z, :], 0, 0, 2, (grp, blk + 1))),
                (not_first_x, not_last_x, deep_send(eps_in.at[0], EP.at[past, own_z, :], 0, 0, 3, (grp, blk - 1))),
            ]

        def piece(j):
            return slice(j * nz, (j + 1) * nz)

        line = slice(4 * nz, 4 * nz + 1)

        def next_z(v):
            return jnp.where(row == nz - 1, 0.0, pltpu.roll(v, nz - 1, 0))

        def last_z_of(v, edge):
            return jnp.where(row == 0, edge, pltpu.roll(v, 1, 0))

        def next_y(v):
            return jnp.where(lane == ny - 1, 0.0, pltpu.roll(v, ny - 1, 1))

        def last_y(v):
            return jnp.where(lane == 0, 0.0, pltpu.roll(v, 1, 1))

        def partials(q, r):
            k, rate, short = 2 * r, rates[q], (q, r) == (1, 1)

            def h_at(i, over):
                ex, ey, ez = (E[q, k, c, i, own_z, :] for c in range(3))
                oy, oz = (E[q, k, c, i + 1, own_z, :] for c in (1, 2)) if over else (0.0, 0.0)
                hx, hy, hz = (H[q, k, c, i, own_z, :] for c in range(3))
                hx = hx - rate * ((next_y(ez) - ez) - (next_z(ey) - ey))
                hy = hy - rate * ((next_z(ex) - ex) - (oz - ez))
                hz = hz - rate * ((oy - ey) - (next_y(ex) - ex))
                return (ex, ey, ez), (hx, hy, hz)

            def z_edges(e):
                c = jnp.where(first_z, 0.0, rate)
                return c * e[1][0:1, :], -c * e[0][0:1, :]

            e, h = h_at(past - 1, False)
            pu[q, r, piece(0)] = h[1]
            pu[q, r, piece(1)] = h[2]
            if short:
                pd[q, r, piece(0)] = E[q, k, 1, first, own_z, :]
                pd[q, r, piece(1)] = E[q, k, 2, first, own_z, :]
                return
            _, under = h_at(past - 2, True)
            edge_x, edge_y = z_edges(e)
            scale = rate * EP[past - 1, own_z, :]
            ex = e[0] + scale * ((h[2] - last_y(h[2])) - (h[1] - last_z_of(h[1], edge_y)))
            ey = e[1] + scale * ((h[0] - last_z_of(h[0], edge_x)) - (h[2] - under[2]))
            ez = e[2] + scale * ((h[1] - under[1]) - (h[0] - last_y(h[0])))
            pu[q, r, piece(2)] = h[1] - rate * ((next_z(ex) - ex) + ez)
            pu[q, r, piece(3)] = h[2] + rate * (ey + (next_y(ex) - ex))
            pu[q, r, line] = edge_y

            e, h = h_at(first, True)
            edge_x, edge_y = z_edges(e)
            scale = rate * EP[first, own_z, :]
            pd[q, r, piece(0)] = e[1]
            pd[q, r, piece(1)] = e[2]
            pd[q, r, piece(2)] = e[1] + scale * ((h[0] - last_z_of(h[0], edge_x)) - h[2])
            pd[q, r, piece(3)] = e[2] + scale * (h[1] - (h[0] - last_y(h[0])))
            pd[q, r, line] = edge_y

        def adjoint_half(k):
            vx, vy, vz = (G[k, c, nx, top:end, :] for c in range(3))
            cy, cz = half_curl(vx, vy, vz, G[k, 0, nx, top + 1:end + 1, :])
            qa[k, 0] = AH[q, k, 1, nx, top:end, :] + rate * cy
            qa[k, 1] = AH[q, k, 2, nx, top:end, :] + rate * cz

        def z_links(q, r):
            nu, nd = z_rows[q, r]
            jobs = [
                (not_last_z, not_first_z, deep_send(zus.at[q, r, 0:nu], zur.at[q, r, 0:nu], q, r, 4, (grp + 1, blk))),
                (not_first_z, not_last_z, deep_send(zds.at[q, r, 0:nd], zdr.at[q, r, 0:nd], q, r, 5, (grp - 1, blk))),
            ]
            has = {1: (not_last_z, not_first_z), -1: (not_first_z, not_last_z)}
            has_x = {1: (not_last_x, not_first_x), -1: (not_first_x, not_last_x)}
            for j, (dg, db, _) in enumerate(corners):
                jobs.append((
                    both(has[dg][0], has_x[db][0]), both(has[dg][1], has_x[db][1]),
                    deep_send(cs.at[q, r, j], cr.at[q, r, j], q, r, 6 + j, (grp + dg, blk + db))))
            return jobs

        def pack(q, r):
            k = 2 * r
            for table, buf, count in zip((z_up, z_dn), (zus, zds), z_rows[q, r]):
                for j, (name, c, at, _) in enumerate(table[0:count]):
                    ref = part_of(name, q, k)(c)
                    for i in range(nx):
                        buf[q, r, j, i] = ref[i + first, at:at + 1, :]
            for m, (_, _, rows) in enumerate(corners):
                for j, (name, c, layer, _, at, _) in enumerate(rows):
                    if name != "p" or (q, r) == (0, 0):
                        cs[q, r, m, j] = part_of(name, q, k)(c)[layer, at:at + 1, :]

        def unpack(q, r):
            k = 2 * r
            for table, buf, cond, count in zip((z_up, z_dn), (zur, zdr), (not_first_z, not_last_z), z_rows[q, r]):
                @pl.when(cond)
                def _(table=table, buf=buf, count=count):
                    for j, (name, c, _, at) in enumerate(table[0:count]):
                        ref = part_of(name, q, k)(c)
                        for i in range(nx):
                            ref[i + first, at:at + 1, :] = buf[q, r, j, i]
            for m, (job, (_, _, rows)) in enumerate(zip(z_links(q, r)[2:], corners)):
                @pl.when(job[1])
                def _(m=m, rows=rows):
                    for j, (name, c, _, layer, _, at) in enumerate(rows):
                        if name != "p" or (q, r) == (0, 0):
                            part_of(name, q, k)(c)[layer, at:at + 1, :] = cr[q, r, m, j]
            unpack_x(q, r)

        def unpack_x(q, r):
            k = 2 * r
            for c in (1, 2):
                E[q, k, c, spare, lo:pad, :] = E[q, k, c, past, lo:pad, :]
                E[q, k, c, spare, own_z, :] = pdr[q, r, piece(c - 1)]
                E[q, k, c, spare, deep:hi, :] = E[q, k, c, past, deep:hi, :]

            @pl.when(last_x)
            def _():
                E[q, k, :, spare, lo:hi, :] = jnp.zeros((3, hi - lo, ny), jnp.float32)

        def start(jobs):
            for sends, _, copy in jobs:
                used.append((sends, copy))
                pl.when(sends)(copy.start)

        def finish(jobs):
            for _, gets, copy in jobs:
                pl.when(gets)(copy.wait_recv)

        def curl_up(buf, i, r0, r1, above):
            vx, vy, vz = (buf[c, i, r0:r1, :] for c in range(3))
            last = lane_d[0:r1 - r0] == ny - 1

            def dy(v):
                return jnp.where(last, 0.0, pltpu.roll(v, ny - 1, 1)) - v

            dxy, dxz = (buf[c, above, r0:r1, :] - v for c, v in ((1, vy), (2, vz)))
            dzx, dzy = (buf[c, i, r0 + 1:r1 + 1, :] - v for c, v in ((0, vx), (1, vy)))
            return dy(vz) - dzy, dzx - dxz, dxy - dy(vx)

        def curl_dn(buf, i, r0, r1, below):
            vx, vy, vz = (buf[c, i, r0:r1, :] for c in range(3))
            head = lane_d[0:r1 - r0] == 0

            def dy(v):
                return v - jnp.where(head, 0.0, pltpu.roll(v, 1, 1))

            dxy, dxz = (v - buf[c, below, r0:r1, :] for c, v in ((1, vy), (2, vz)))
            dzx, dzy = (v - buf[c, i, r0 - 1:r1 - 1, :] for c, v in ((0, vx), (1, vy)))
            return dy(vz) - dzy, dzx - dxz, dxy - dy(vx)

        def h_step(q, k, r1):
            r, rate, last = k // 2, rates[q], (q, k) == (1, 2)

            def body(i, to=None, above=None):
                cv = curl_up(E.at[q, k], i, lo, r1, i + 1 if above is None else above)
                to = i if to is None else to
                for c in range(3):
                    new = H[q, k, c, i, lo:r1, :] - rate * cv[c]
                    H[q, k + 1, c, to, lo:r1, :] = new
                    if (q, k) == (0, steps - 1) and to is i:
                        h_out[c, i - first] = new[8:8 + nz]

            wide = k % 2 == 0
            body(first - 1, None if wide else spare)
            each(first, past - 1, body)
            body(past - 1, None, spare)
            if wide:
                if not last:
                    body(past)
                edge = -rate * E[q, k, 0, 0, deep:deep + 1, :]
                H[q, k + 1, 1, 0, deep - 1:deep, :] = edge
                for c in (1, 2):
                    H[q, k + 1, c, spare, lo:pad, :] = H[q, k + 1, c, 1, lo:pad, :]
                    H[q, k + 1, c, spare, own_z, :] = H[q, k + 1, c, 1, own_z, :] + pur[q, r, piece(c - 1)]
                    if r1 > deep:
                        H[q, k + 1, c, spare, deep:r1, :] = H[q, k + 1, c, 1, deep:r1, :]
                if not last:
                    H[q, k + 1, 1, spare, pad - 1:pad, :] = H[q, k + 1, 1, spare, pad - 1:pad, :] + pur[q, r, line]
            else:
                for c in (1, 2):
                    H[q, k + 1, c, spare, own_z, :] = H[q, k + 1, c, spare, own_z, :] + pur[q, r, piece(c + 1)]

            @pl.when(first_x)
            def _():
                for i in (0, 1, spare) if wide else (spare,):
                    H[q, k + 1, :, i, lo:r1, :] = jnp.zeros((3, r1 - lo, ny), jnp.float32)

            @pl.when(first_z)
            def _():
                for i in [*range(first - 1, past + 1), spare] if wide else range(first, past):
                    H[q, k + 1, :, i, lo:pad, :] = jnp.zeros((3, pad - lo, ny), jnp.float32)

        def keep_curl(q, k, i, cv):
            term = 0.0
            for c in range(3):
                if q:
                    new = AE[k, c, i] - COURANT * cv[c]
                    if k < 2:
                        AE[k + 1, c, i] = new
                    term = term + new * CURL[2 - k, c, i] if k else term
                elif k < 2:
                    CURL[k, c, i] = cv[c]
                else:
                    term = term + AE[steps - 1 - k, c, i] * cv[c]
            if (q, k) == (1, 1):
                GR[i] = term
            elif k > 1:
                GR[i] = GR[i] + term

        def e_wide(q, k):
            r, rate = k // 2, rates[q]

            def outer(i, below=None):
                cv = curl_dn(H.at[q, k + 1], i, lo, hi, i - 1 if below is None else below)
                scale = rate * EP[i, lo:hi, :]
                for c in range(3):
                    E[q, k + 1, c, i, lo:hi, :] = E[q, k, c, i, lo:hi, :] + scale * cv[c]
                return cv

            def inner(i, below=None):
                cv = [v[8:8 + nz] for v in outer(i, below)]
                keep_curl(q, k, i - first, cv)

            outer(first - 1)
            inner(first, spare)
            each(first + 1, past, inner)
            outer(past)
            edge = rate * EP[1, deep:deep + 1, :] * pur[q, r, nz - 1:nz]
            E[q, k + 1, 0, 1, deep:deep + 1, :] = E[q, k + 1, 0, 1, deep:deep + 1, :] + edge
            ey = rate * pdr[q, r, 0:1]
            edge = pdr[q, r, line] - (ey - jnp.where(lane[0:1] == 0, 0.0, pltpu.roll(ey, 1, 1)))
            edge = rate * EP[past, pad - 1:pad, :] * edge
            E[q, k + 1, 2, past, pad - 1:pad, :] = E[q, k + 1, 2, past, pad - 1:pad, :] + edge
            for c in (1, 2):
                E[q, k + 1, c, spare, lo:pad, :] = E[q, k + 1, c, past, lo:pad, :]
                E[q, k + 1, c, spare, own_z, :] = E[q, k + 1, c, past, own_z, :] + pdr[q, r, piece(c + 1)]
                E[q, k + 1, c, spare, deep:hi, :] = E[q, k + 1, c, past, deep:hi, :]

            @pl.when(last_x)
            def _():
                for i in (past, spare):
                    E[q, k + 1, :, i, lo:hi, :] = jnp.zeros((3, hi - lo, ny), jnp.float32)

            @pl.when(last_z)
            def _():
                for i in [*range(first - 1, past + 1), spare]:
                    E[q, k + 1, :, i, deep:hi, :] = jnp.zeros((3, hi - deep, ny), jnp.float32)

        def e_own(q, k, dst):
            rate = rates[q]

            def body(i, below=None):
                cv = curl_dn(H.at[q, k + 1], i, pad, deep, i - 1 if below is None else below)
                scale = rate * eps[i - first]
                keep_curl(q, k, i - first, cv)
                for c in range(3):
                    dst(c, i, E[q, k, c, i, own_z, :] + scale * cv[c])
            return body

        def adjoint_last():
            def body(i, below=None):
                keep_curl(1, 2, i - first, curl_dn(H.at[1, 3], i, pad, deep, i - 1 if below is None else below))

            body(first, spare)
            each(first + 1, past, body)

        def first_g(i):
            for c in range(3):
                E[1, 0, c, i, own_z, :] = eps[i - first] * AE[0, c, i - first]

        for j in (2, 3, 6):
            loads[j].wait()
        partials(0, 0)
        pl.semaphore_wait(barrier, near_by)
        start(x_links(0, 0))
        start(eps_links())
        for j in (1, 0, 4):
            loads[j].wait()
        for i in (first, first + 1, past - 2, past - 1):
            first_g(i)
        partials(1, 0)
        start(x_links(1, 0))
        pack(0, 0)
        start(z_links(0, 0))
        each(first + 2, past - 2, first_g)
        pack(1, 0)
        start(z_links(1, 0))
        for s in range(len(stages))[:1]:
            tell(s)
        loads[5].wait()

        own = lax.broadcasted_iota(jnp.int32, (n, ny), 0)
        place = lax.broadcasted_iota(jnp.int32, (VOX_DEV, ny), 0)

        def hits(i, z):
            high = ids[i, z:z + 1, :] // VOX_DEV
            return jnp.where(high == own, 1.0, 0.0).astype(jnp.bfloat16)

        def prepare(i):
            low = ids[i] % VOX_DEV
            for z in range(nz):
                cols = slice(z * ny, (z + 1) * ny)
                low_hot[i, :, cols] = jnp.where(low[z:z + 1, :] == place, 1.0, 0.0).astype(jnp.bfloat16)
                if stored:
                    high_hot[i, :, cols] = hits(i, z)

        each(0, nx, prepare)

        def two_steps(q, r, dst, after=None):
            k = 2 * r
            finish(x_links(q, r) + z_links(q, r))
            unpack(q, r)
            h_step(q, k, hi)
            e_wide(q, k)
            h_step(q, k + 1, deep)
            body = e_own(q, k + 1, dst)
            body(first, spare)
            if r:
                each(first + 1, past, body)
                return
            for i in (first + 1, past - 2, past - 1):
                body(i)
            partials(q, 1)
            start(x_links(q, 1))
            each(first + 2, past - 2, body)
            pack(q, 1)
            start(z_links(q, 1))

        def pass_on(s):
            if s < len(stages):
                hear(s)
                if s + 1 < len(stages):
                    tell(s + 1)

        def to_next(q):
            def put(c, i, new):
                E[q, 2, c, i, own_z, :] = new
            return put

        def to_out(c, i, new):
            e_out[c, i - first] = new

        finish(eps_links())
        two_steps(0, 0, to_next(0))
        pass_on(0)
        two_steps(1, 0, to_next(1))
        pass_on(1)
        two_steps(0, 1, to_out)
        pass_on(2)
        finish(x_links(1, 1) + z_links(1, 1))
        unpack(1, 1)
        h_step(1, 2, deep)
        adjoint_last()

        part[...] = jnp.zeros_like(part)

        def seg(i):
            grad = COURANT * GR[i]
            coarse = grad.astype(jnp.bfloat16).astype(jnp.float32)
            fine = grad - coarse
            lhs = []
            for z in range(nz):
                hit = high_hot[i, :, z * ny:(z + 1) * ny] if stored else hits(i, z)
                cells = []
                for v in (coarse, fine):
                    line = jnp.broadcast_to(v[z:z + 1, :], (16, ny)).astype(jnp.bfloat16)
                    cells += [hit[q:q + 16] * line for q in range(0, n, 16)]
                lhs.append(jnp.concatenate(cells, axis=0))
            part[...] += lax.dot_general(
                jnp.concatenate(lhs, axis=1), low_hot[i],
                (((1,), (1,)), ((), ())), preferred_element_type=jnp.float32)

        each(0, nx, seg)

        total = part[0:n, :] + part[n:2 * n, :]
        total = jnp.concatenate([total, jnp.zeros((n, 128 - VOX_DEV), jnp.float32)], axis=1)
        for d in range(n):
            S[d] = total[d:d + 1, :]

        for s in range(3, len(stages)):
            pass_on(s)

        for dg in reversed(range(ng)):
            to_grp = (grp + dg) % ng

            def send_row(db, carry, to_grp=to_grp):
                to_blk = blk ^ (nb - 1 - db) if nb & (nb - 1) == 0 else (blk + nb - 1 - db) % nb
                pltpu.make_async_remote_copy(
                    S.at[to_grp * nb + to_blk], R.at[me], as_sem, ar_sem,
                    device_id=(to_grp, to_blk), device_id_type=MESH).start()
                return carry

            lax.fori_loop(0, nb if dg else nb - 1, send_row, 0, unroll=True)

        R[me] = S[me]
        rest = pl.ds(0, n - 1)
        pltpu.make_async_copy(R.at[rest], R.at[rest], ar_sem).wait()
        v_out[...] = jnp.sum(R[...], axis=0)[:, 0:VOX_DEV]
        pltpu.make_async_copy(S.at[rest], S.at[rest], as_sem).wait()
        for sends, copy in used:
            pl.when(sends)(copy.wait_send)

    return kernel


def write_out(e_in, h_in, v_in, e_out, h_out, v_out, sem):
    copies = [
        pltpu.make_async_copy(a.at[c], b.at[c], sem.at[3 * j + c])
        for j, (a, b) in enumerate(((e_in, e_out), (h_in, h_out))) for c in range(3)
    ] + [pltpu.make_async_copy(v_in, v_out, sem.at[6])]
    for copy in copies:
        copy.start()
    for copy in copies:
        copy.wait()


def solution(mesh):
    ng, nb = mesh.shape["grp"], mesh.shape["blk"]
    n = ng * nb

    def local(e_field, h_field, inv_eps, cot_e, cot_h, voxel_ids):
        _, nx, nz, ny = e_field.shape
        f32 = jnp.float32
        plain = (3, nx, nz, ny)
        deep = (3, nx + 5, nz + 40, ny)
        dma = pltpu.SemaphoreType.DMA
        hbm = pl.BlockSpec(memory_space=pl.ANY)
        vmem = pl.BlockSpec(memory_space=pltpu.VMEM)
        e_new, h_new, vox = pl.pallas_call(
            make_kernel(ng, nb, nx, nz, ny),
            out_shape=(
                pltpu.VMEM(plain, f32),
                pltpu.VMEM(plain, f32),
                pltpu.VMEM((1, VOX_DEV), f32),
            ),
            in_specs=[hbm] * 6,
            out_specs=(vmem,) * 3,
            scratch_shapes=[
                pltpu.VMEM((2, STEPS) + deep, f32),
                pltpu.VMEM((2, STEPS + 1) + deep, f32),
                pltpu.VMEM(deep[1:], f32),
                pltpu.VMEM((2, 2, 4 * nz + 8, ny), f32),
                pltpu.VMEM((2, 2, 4 * nz + 8, ny), f32),
                pltpu.VMEM((2, 2, 4 * nz + 8, ny), f32),
                pltpu.VMEM((2, 2, 4 * nz + 8, ny), f32),
                pltpu.VMEM((2, 2, 12, nx, 1, ny), f32),
                pltpu.VMEM((2, 2, 12, nx, 1, ny), f32),
                pltpu.VMEM((2, 2, 9, nx, 1, ny), f32),
                pltpu.VMEM((2, 2, 9, nx, 1, ny), f32),
                pltpu.VMEM((2, 2, 4, 8, 1, ny), f32),
                pltpu.VMEM((2, 2, 4, 8, 1, ny), f32),
                pltpu.VMEM((3,) + plain, f32),
                pltpu.VMEM((2,) + plain, f32),
                pltpu.VMEM(plain[1:], f32),
                pltpu.VMEM(plain[1:], jnp.int32),
                pltpu.VMEM(plain[1:], f32),
                pltpu.VMEM((nx, VOX_DEV, nz * ny), jnp.bfloat16),
                pltpu.VMEM((nx, n if n <= STORED else 16, nz * ny), jnp.bfloat16),
                pltpu.VMEM((n, 1, 128), f32),
                pltpu.VMEM((n, 1, 128), f32),
                pltpu.VMEM((2 * n, VOX_DEV), f32),
                dma((7,)), dma, dma, dma((2, 2, 10)), dma((2, 2, 10)),
                pltpu.SemaphoreType.REGULAR((max(1, len(spread(nb))),)),
            ],
            compiler_params=pltpu.CompilerParams(
                collective_id=0, has_side_effects=True, vmem_limit_bytes=LIMIT),
        )(e_field, h_field, inv_eps, cot_e, cot_h, voxel_ids)
        e_new, h_new, vox = pl.pallas_call(
            write_out,
            out_shape=(
                jax.ShapeDtypeStruct(plain, f32),
                jax.ShapeDtypeStruct(plain, f32),
                jax.ShapeDtypeStruct((1, VOX_DEV), f32),
            ),
            in_specs=[hbm, hbm, hbm],
            out_specs=(hbm, hbm, hbm),
            scratch_shapes=[dma((7,))],
            compiler_params=pltpu.CompilerParams(vmem_limit_bytes=1024 * 1024),
        )(e_new, h_new, vox)
        return e_new, h_new, vox.reshape(VOX_DEV)

    field, cell = P(None, "blk", "grp", None), P("blk", "grp", None)
    return jax.shard_map(
        local, mesh=mesh,
        in_specs=(field, field, cell, field, field, cell),
        out_specs=(field, field, P(("grp", "blk"))),
        check_vma=False,
    )
```

```python
import jax
import jax.numpy as jnp
from jax import lax
from jax.experimental import pallas as pl
from jax.experimental.pallas import tpu as pltpu
from jax.sharding import PartitionSpec as P

STEPS = 4
COURANT = 0.5
MESH = pl.DeviceIdType.MESH
VOX_DEV = 64
STORED = 64
REACH = 1
UNROLL = True
LIMIT = 60 * 1024 * 1024


def spread(nb):
    stages, reach = [], REACH
    while reach < nb - 1:
        stages.append(reach)
        reach *= 2
    return stages


def make_kernel(ng, nb, nx, nz, ny):
    n = ng * nb
    steps = STEPS
    stored = n <= STORED
    stages = spread(nb)
    pad, deep = 16, 16 + nz
    lo, hi = pad - 8, deep + 8
    first, past, spare = 2, nx + 2, nx + 4
    z_up = [(a, c, deep - 1, pad - 1) for a in ("e", "h") for c in range(3)]
    z_up += [("e", c, deep - 2, pad - 2) for c in range(3)] + [("h", c, deep - 2, pad - 2) for c in range(2)]
    z_up += [("p", 0, deep - 1, pad - 1)]
    z_dn = [("e", c, pad, deep) for c in range(3)] + [("e", c, pad + 1, deep + 1) for c in range(2)]
    z_dn += [("h", c, pad, deep) for c in range(3)] + [("p", 0, pad, deep)]
    z_rows = {(0, 0): (12, 9), (0, 1): (11, 8), (1, 0): (11, 8), (1, 1): (6, 3)}
    near, far = (past - 1, first - 1), (first, past)
    corners = [
        (1, -1, [("e", c, *far, deep - 1, pad - 1) for c in range(3)]
         + [("e", 2, first + 1, past + 1, deep - 1, pad - 1), ("e", 2, *far, deep - 2, pad - 2)]
         + [("h", c, *far, deep - 1, pad - 1) for c in range(2)] + [("p", 0, *far, deep - 1, pad - 1)]),
        (1, 1, [(a, c, *near, deep - 1, pad - 1) for a in ("e", "h") for c in range(3)]),
        (-1, 1, [("e", c, *near, pad, deep) for c in range(3)]
         + [("e", 0, *near, pad + 1, deep + 1), ("e", 0, past - 2, first - 2, pad, deep)]
         + [("h", c, *near, pad, deep) for c in (1, 2)] + [("p", 0, *near, pad, deep)]),
        (-1, -1, [("e", c, *far, pad, deep) for c in range(3)]),
    ]

    def kernel(e_in, h_in, eps_in, ce_in, ch_in, ids_in, e_out, h_out, v_out,
               E, H, EP, pu, pur, pd, pdr, zus, zur, zds, zdr, cs, cr,
               AE, CURL, eps, ids,
               GR, low_hot, high_hot, S, R, part, in_sem, as_sem, ar_sem, fs_sem, fr_sem, known):
        grp = lax.axis_index("grp")
        blk = lax.axis_index("blk")
        me = grp * nb + blk
        lane = lax.broadcasted_iota(jnp.int32, (nz, ny), 1)
        row = lax.broadcasted_iota(jnp.int32, (nz, ny), 0)
        lane_d = lax.broadcasted_iota(jnp.int32, (hi - lo, ny), 1)

        own_x, own_z = slice(first, past), slice(pad, deep)
        loads = [
            pltpu.make_async_copy(ce_in, AE.at[0], in_sem.at[0]),
            pltpu.make_async_copy(eps_in, eps, in_sem.at[1]),
            pltpu.make_async_copy(e_in, E.at[0, 0, :, own_x, own_z, :], in_sem.at[2]),
            pltpu.make_async_copy(h_in, H.at[0, 0, :, own_x, own_z, :], in_sem.at[3]),
            pltpu.make_async_copy(ch_in, H.at[1, 0, :, own_x, own_z, :], in_sem.at[4]),
            pltpu.make_async_copy(ids_in, ids, in_sem.at[5]),
            pltpu.make_async_copy(eps_in, EP.at[own_x, own_z, :], in_sem.at[6]),
        ]
        for j in (2, 3, 6, 1, 0, 4, 5):
            loads[j].start()

        barrier = pltpu.get_barrier_semaphore()

        for db in range(-REACH, REACH + 1):
            for dg in range(ng):
                if db or dg:
                    @pl.when(jnp.logical_and(blk + db >= 0, blk + db < nb))
                    def _(db=db, dg=dg):
                        pl.semaphore_signal(
                            barrier, inc=1, device_id=((grp + dg) % ng, blk + db), device_id_type=MESH)

        near_by = ng * (jnp.minimum(blk + REACH, nb - 1) - jnp.maximum(blk - REACH, 0) + 1) - 1

        def tell(s):
            for d in (-stages[s], stages[s]):
                @pl.when(jnp.logical_and(blk + d >= 0, blk + d < nb))
                def _(d=d):
                    pl.semaphore_signal(known.at[s], inc=1, device_id=(grp, blk + d), device_id_type=MESH)

        def hear(s):
            d = stages[s]
            pl.semaphore_wait(known.at[s], jnp.where(blk >= d, 1, 0) + jnp.where(blk + d < nb, 1, 0))

        first_x, last_x = blk == 0, blk == nb - 1
        first_z, last_z = grp == 0, grp == ng - 1
        not_first_x, not_last_x = jnp.logical_not(first_x), jnp.logical_not(last_x)
        not_first_z, not_last_z = jnp.logical_not(first_z), jnp.logical_not(last_z)
        both = jnp.logical_and

        starts = [(q, k) for q in range(2) for k in (0, 2)]
        for q, k in starts:
            for i in (1, past, past + 1):
                E[q, k, :, i, own_z, :] = jnp.zeros((3, nz, ny), jnp.float32)
            for i in (1, past):
                H[q, k, :, i, own_z, :] = jnp.zeros((3, nz, ny), jnp.float32)
            H[q, k + 1, 1:3, 0, own_z, :] = jnp.zeros((2, nz, ny), jnp.float32)

        @pl.when(last_x)
        def _():
            for q, k in starts:
                E[q, k, :, past, lo:hi, :] = jnp.zeros((3, hi - lo, ny), jnp.float32)

        @pl.when(last_z)
        def _():
            for q, k in starts:
                E[q, k, :, 0:nx + 4, deep:hi, :] = jnp.zeros((3, nx + 4, hi - deep, ny), jnp.float32)

        used = []

        def each(start, stop, body):
            def step(i, carry):
                body(i)
                return carry
            lax.fori_loop(start, stop, step, 0, unroll=UNROLL)

        rates = (COURANT, -COURANT)
        def part_of(name, q, k):
            return {"e": lambda c: E.at[q, k, c], "h": lambda c: H.at[q, k, c], "p": lambda c: EP}[name]

        def deep_send(src, dst, q, r, slot, to):
            return pltpu.make_async_remote_copy(
                src, dst, fs_sem.at[q, r, slot], fr_sem.at[q, r, slot], device_id=to, device_id_type=MESH)

        def x_links(q, r):
            up, dn = (grp, blk + 1), (grp, blk - 1)
            rows = slice(0, 2 * nz if (q, r) == (1, 1) else 4 * nz + 8)
            ups = [deep_send(pu.at[q, r, rows], pur.at[q, r, rows], q, r, 0, up)]
            dns = [deep_send(pd.at[q, r, rows], pdr.at[q, r, rows], q, r, 1, dn)]
            return [(not_last_x, not_first_x, copy) for copy in ups] + [(not_first_x, not_last_x, copy) for copy in dns]

        def eps_links():
            return [
                (not_last_x, not_first_x, deep_send(eps_in.at[nx - 1], EP.at[1, own_z, :], 0, 0, 2, (grp, blk + 1))),
                (not_first_x, not_last_x, deep_send(eps_in.at[0], EP.at[past, own_z, :], 0, 0, 3, (grp, blk - 1))),
            ]

        def piece(j):
            return slice(j * nz, (j + 1) * nz)

        line = slice(4 * nz, 4 * nz + 1)

        def next_z(v):
            return jnp.where(row == nz - 1, 0.0, pltpu.roll(v, nz - 1, 0))

        def last_z_of(v, edge):
            return jnp.where(row == 0, edge, pltpu.roll(v, 1, 0))

        def next_y(v):
            return jnp.where(lane == ny - 1, 0.0, pltpu.roll(v, ny - 1, 1))

        def last_y(v):
            return jnp.where(lane == 0, 0.0, pltpu.roll(v, 1, 1))

        def partials(q, r):
            k, rate, short = 2 * r, rates[q], (q, r) == (1, 1)

            def h_at(i, over):
                ex, ey, ez = (E[q, k, c, i, own_z, :] for c in range(3))
                oy, oz = (E[q, k, c, i + 1, own_z, :] for c in (1, 2)) if over else (0.0, 0.0)
                hx, hy, hz = (H[q, k, c, i, own_z, :] for c in range(3))
                hx = hx - rate * ((next_y(ez) - ez) - (next_z(ey) - ey))
                hy = hy - rate * ((next_z(ex) - ex) - (oz - ez))
                hz = hz - rate * ((oy - ey) - (next_y(ex) - ex))
                return (ex, ey, ez), (hx, hy, hz)

            def z_edges(e):
                c = jnp.where(first_z, 0.0, rate)
                return c * e[1][0:1, :], -c * e[0][0:1, :]

            e, h = h_at(past - 1, False)
            pu[q, r, piece(0)] = h[1]
            pu[q, r, piece(1)] = h[2]
            if short:
                pd[q, r, piece(0)] = E[q, k, 1, first, own_z, :]
                pd[q, r, piece(1)] = E[q, k, 2, first, own_z, :]
                return
            _, under = h_at(past - 2, True)
            edge_x, edge_y = z_edges(e)
            scale = rate * EP[past - 1, own_z, :]
            ex = e[0] + scale * ((h[2] - last_y(h[2])) - (h[1] - last_z_of(h[1], edge_y)))
            ey = e[1] + scale * ((h[0] - last_z_of(h[0], edge_x)) - (h[2] - under[2]))
            ez = e[2] + scale * ((h[1] - under[1]) - (h[0] - last_y(h[0])))
            pu[q, r, piece(2)] = h[1] - rate * ((next_z(ex) - ex) + ez)
            pu[q, r, piece(3)] = h[2] + rate * (ey + (next_y(ex) - ex))
            pu[q, r, line] = edge_y

            e, h = h_at(first, True)
            edge_x, edge_y = z_edges(e)
            scale = rate * EP[first, own_z, :]
            pd[q, r, piece(0)] = e[1]
            pd[q, r, piece(1)] = e[2]
            pd[q, r, piece(2)] = e[1] + scale * ((h[0] - last_z_of(h[0], edge_x)) - h[2])
            pd[q, r, piece(3)] = e[2] + scale * (h[1] - (h[0] - last_y(h[0])))
            pd[q, r, line] = edge_y

        def adjoint_half(k):
            vx, vy, vz = (G[k, c, nx, top:end, :] for c in range(3))
            cy, cz = half_curl(vx, vy, vz, G[k, 0, nx, top + 1:end + 1, :])
            qa[k, 0] = AH[q, k, 1, nx, top:end, :] + rate * cy
            qa[k, 1] = AH[q, k, 2, nx, top:end, :] + rate * cz

        def z_links(q, r):
            nu, nd = z_rows[q, r]
            jobs = [
                (not_last_z, not_first_z, deep_send(zus.at[q, r, 0:nu], zur.at[q, r, 0:nu], q, r, 4, (grp + 1, blk))),
                (not_first_z, not_last_z, deep_send(zds.at[q, r, 0:nd], zdr.at[q, r, 0:nd], q, r, 5, (grp - 1, blk))),
            ]
            has = {1: (not_last_z, not_first_z), -1: (not_first_z, not_last_z)}
            has_x = {1: (not_last_x, not_first_x), -1: (not_first_x, not_last_x)}
            for j, (dg, db, _) in enumerate(corners):
                jobs.append((
                    both(has[dg][0], has_x[db][0]), both(has[dg][1], has_x[db][1]),
                    deep_send(cs.at[q, r, j], cr.at[q, r, j], q, r, 6 + j, (grp + dg, blk + db))))
            return jobs

        def pack(q, r):
            k = 2 * r
            for table, buf, count in zip((z_up, z_dn), (zus, zds), z_rows[q, r]):
                for j, (name, c, at, _) in enumerate(table[0:count]):
                    ref = part_of(name, q, k)(c)
                    for i in range(nx):
                        buf[q, r, j, i] = ref[i + first, at:at + 1, :]
            for m, (_, _, rows) in enumerate(corners):
                for j, (name, c, layer, _, at, _) in enumerate(rows):
                    if name != "p" or (q, r) == (0, 0):
                        cs[q, r, m, j] = part_of(name, q, k)(c)[layer, at:at + 1, :]

        def unpack(q, r):
            k = 2 * r
            for table, buf, cond, count in zip((z_up, z_dn), (zur, zdr), (not_first_z, not_last_z), z_rows[q, r]):
                @pl.when(cond)
                def _(table=table, buf=buf, count=count):
                    for j, (name, c, _, at) in enumerate(table[0:count]):
                        ref = part_of(name, q, k)(c)
                        for i in range(nx):
                            ref[i + first, at:at + 1, :] = buf[q, r, j, i]
            for m, (job, (_, _, rows)) in enumerate(zip(z_links(q, r)[2:], corners)):
                @pl.when(job[1])
                def _(m=m, rows=rows):
                    for j, (name, c, _, layer, _, at) in enumerate(rows):
                        if name != "p" or (q, r) == (0, 0):
                            part_of(name, q, k)(c)[layer, at:at + 1, :] = cr[q, r, m, j]
            unpack_x(q, r)

        def unpack_x(q, r):
            k = 2 * r
            for c in (1, 2):
                E[q, k, c, spare, lo:pad, :] = E[q, k, c, past, lo:pad, :]
                E[q, k, c, spare, own_z, :] = pdr[q, r, piece(c - 1)]
                E[q, k, c, spare, deep:hi, :] = E[q, k, c, past, deep:hi, :]

            @pl.when(last_x)
            def _():
                E[q, k, :, spare, lo:hi, :] = jnp.zeros((3, hi - lo, ny), jnp.float32)

        def start(jobs):
            for sends, _, copy in jobs:
                used.append((sends, copy))
                pl.when(sends)(copy.start)

        def finish(jobs):
            for _, gets, copy in jobs:
                pl.when(gets)(copy.wait_recv)

        def curl_up(buf, i, r0, r1, above):
            vx, vy, vz = (buf[c, i, r0:r1, :] for c in range(3))
            last = lane_d[0:r1 - r0] == ny - 1

            def dy(v):
                return jnp.where(last, 0.0, pltpu.roll(v, ny - 1, 1)) - v

            dxy, dxz = (buf[c, above, r0:r1, :] - v for c, v in ((1, vy), (2, vz)))
            dzx, dzy = (buf[c, i, r0 + 1:r1 + 1, :] - v for c, v in ((0, vx), (1, vy)))
            return dy(vz) - dzy, dzx - dxz, dxy - dy(vx)

        def curl_dn(buf, i, r0, r1, below):
            vx, vy, vz = (buf[c, i, r0:r1, :] for c in range(3))
            head = lane_d[0:r1 - r0] == 0

            def dy(v):
                return v - jnp.where(head, 0.0, pltpu.roll(v, 1, 1))

            dxy, dxz = (v - buf[c, below, r0:r1, :] for c, v in ((1, vy), (2, vz)))
            dzx, dzy = (v - buf[c, i, r0 - 1:r1 - 1, :] for c, v in ((0, vx), (1, vy)))
            return dy(vz) - dzy, dzx - dxz, dxy - dy(vx)

        def h_step(q, k, r1):
            r, rate, last = k // 2, rates[q], (q, k) == (1, 2)

            def body(i, to=None, above=None):
                cv = curl_up(E.at[q, k], i, lo, r1, i + 1 if above is None else above)
                to = i if to is None else to
                for c in range(3):
                    new = H[q, k, c, i, lo:r1, :] - rate * cv[c]
                    H[q, k + 1, c, to, lo:r1, :] = new
                    if (q, k) == (0, steps - 1) and to is i:
                        h_out[c, i - first] = new[8:8 + nz]

            wide = k % 2 == 0
            body(first - 1, None if wide else spare)
            each(first, past - 1, body)
            body(past - 1, None, spare)
            if wide:
                if not last:
                    body(past)
                edge = -rate * E[q, k, 0, 0, deep:deep + 1, :]
                H[q, k + 1, 1, 0, deep - 1:deep, :] = edge
                for c in (1, 2):
                    H[q, k + 1, c, spare, lo:pad, :] = H[q, k + 1, c, 1, lo:pad, :]
                    H[q, k + 1, c, spare, own_z, :] = H[q, k + 1, c, 1, own_z, :] + pur[q, r, piece(c - 1)]
                    if r1 > deep:
                        H[q, k + 1, c, spare, deep:r1, :] = H[q, k + 1, c, 1, deep:r1, :]
                if not last:
                    H[q, k + 1, 1, spare, pad - 1:pad, :] = H[q, k + 1, 1, spare, pad - 1:pad, :] + pur[q, r, line]
            else:
                for c in (1, 2):
                    H[q, k + 1, c, spare, own_z, :] = H[q, k + 1, c, spare, own_z, :] + pur[q, r, piece(c + 1)]

            @pl.when(first_x)
            def _():
                for i in (0, 1, spare) if wide else (spare,):
                    H[q, k + 1, :, i, lo:r1, :] = jnp.zeros((3, r1 - lo, ny), jnp.float32)

            @pl.when(first_z)
            def _():
                for i in [*range(first - 1, past + 1), spare] if wide else range(first, past):
                    H[q, k + 1, :, i, lo:pad, :] = jnp.zeros((3, pad - lo, ny), jnp.float32)

        def keep_curl(q, k, i, cv):
            term = 0.0
            for c in range(3):
                if q:
                    new = AE[k, c, i] - COURANT * cv[c]
                    if k < 2:
                        AE[k + 1, c, i] = new
                    term = term + new * CURL[2 - k, c, i] if k else term
                elif k < 2:
                    CURL[k, c, i] = cv[c]
                else:
                    term = term + AE[steps - 1 - k, c, i] * cv[c]
            if (q, k) == (1, 1):
                GR[i] = term
            elif k > 1:
                GR[i] = GR[i] + term

        def e_wide(q, k):
            r, rate = k // 2, rates[q]

            def outer(i, below=None):
                cv = curl_dn(H.at[q, k + 1], i, lo, hi, i - 1 if below is None else below)
                scale = rate * EP[i, lo:hi, :]
                for c in range(3):
                    E[q, k + 1, c, i, lo:hi, :] = E[q, k, c, i, lo:hi, :] + scale * cv[c]
                return cv

            def inner(i, below=None):
                cv = [v[8:8 + nz] for v in outer(i, below)]
                keep_curl(q, k, i - first, cv)

            outer(first - 1)
            inner(first, spare)
            each(first + 1, past, inner)
            outer(past)
            edge = rate * EP[1, deep:deep + 1, :] * pur[q, r, nz - 1:nz]
            E[q, k + 1, 0, 1, deep:deep + 1, :] = E[q, k + 1, 0, 1, deep:deep + 1, :] + edge
            ey = rate * pdr[q, r, 0:1]
            edge = pdr[q, r, line] - (ey - jnp.where(lane[0:1] == 0, 0.0, pltpu.roll(ey, 1, 1)))
            edge = rate * EP[past, pad - 1:pad, :] * edge
            E[q, k + 1, 2, past, pad - 1:pad, :] = E[q, k + 1, 2, past, pad - 1:pad, :] + edge
            for c in (1, 2):
                E[q, k + 1, c, spare, lo:pad, :] = E[q, k + 1, c, past, lo:pad, :]
                E[q, k + 1, c, spare, own_z, :] = E[q, k + 1, c, past, own_z, :] + pdr[q, r, piece(c + 1)]
                E[q, k + 1, c, spare, deep:hi, :] = E[q, k + 1, c, past, deep:hi, :]

            @pl.when(last_x)
            def _():
                for i in (past, spare):
                    E[q, k + 1, :, i, lo:hi, :] = jnp.zeros((3, hi - lo, ny), jnp.float32)

            @pl.when(last_z)
            def _():
                for i in [*range(first - 1, past + 1), spare]:
                    E[q, k + 1, :, i, deep:hi, :] = jnp.zeros((3, hi - deep, ny), jnp.float32)

        def e_own(q, k, dst):
            rate = rates[q]

            def body(i, below=None):
                cv = curl_dn(H.at[q, k + 1], i, pad, deep, i - 1 if below is None else below)
                scale = rate * eps[i - first]
                keep_curl(q, k, i - first, cv)
                for c in range(3):
                    dst(c, i, E[q, k, c, i, own_z, :] + scale * cv[c])
            return body

        def adjoint_last():
            def body(i, below=None):
                keep_curl(1, 2, i - first, curl_dn(H.at[1, 3], i, pad, deep, i - 1 if below is None else below))

            body(first, spare)
            each(first + 1, past, body)

        def first_g(i):
            for c in range(3):
                E[1, 0, c, i, own_z, :] = eps[i - first] * AE[0, c, i - first]

        for j in (2, 3, 6):
            loads[j].wait()
        partials(0, 0)
        pl.semaphore_wait(barrier, near_by)
        start(x_links(0, 0))
        start(eps_links())
        pack(0, 0)
        start(z_links(0, 0))
        for j in (1, 0, 4):
            loads[j].wait()
        for i in (first, first + 1, past - 2, past - 1):
            first_g(i)
        partials(1, 0)
        start(x_links(1, 0))
        each(first + 2, past - 2, first_g)
        pack(1, 0)
        start(z_links(1, 0))
        for s in range(len(stages))[:1]:
            tell(s)
        loads[5].wait()

        own = lax.broadcasted_iota(jnp.int32, (n, ny), 0)
        place = lax.broadcasted_iota(jnp.int32, (VOX_DEV, ny), 0)

        def hits(i, z):
            high = ids[i, z:z + 1, :] // VOX_DEV
            return jnp.where(high == own, 1.0, 0.0).astype(jnp.bfloat16)

        def prepare(i):
            low = ids[i] % VOX_DEV
            for z in range(nz):
                cols = slice(z * ny, (z + 1) * ny)
                low_hot[i, :, cols] = jnp.where(low[z:z + 1, :] == place, 1.0, 0.0).astype(jnp.bfloat16)
                if stored:
                    high_hot[i, :, cols] = hits(i, z)

        each(0, nx, prepare)

        def two_steps(q, r, dst, after=None):
            k = 2 * r
            finish(x_links(q, r) + z_links(q, r))
            unpack(q, r)
            h_step(q, k, hi)
            e_wide(q, k)
            h_step(q, k + 1, deep)
            body = e_own(q, k + 1, dst)
            body(first, spare)
            if r:
                each(first + 1, past, body)
                return
            for i in (first + 1, past - 2, past - 1):
                body(i)
            partials(q, 1)
            start(x_links(q, 1))
            each(first + 2, past - 2, body)
            pack(q, 1)
            start(z_links(q, 1))

        def pass_on(s):
            if s < len(stages):
                hear(s)
                if s + 1 < len(stages):
                    tell(s + 1)

        def to_next(q):
            def put(c, i, new):
                E[q, 2, c, i, own_z, :] = new
            return put

        def to_out(c, i, new):
            e_out[c, i - first] = new

        finish(eps_links())
        two_steps(0, 0, to_next(0))
        pass_on(0)
        two_steps(1, 0, to_next(1))
        pass_on(1)
        two_steps(0, 1, to_out)
        pass_on(2)
        finish(x_links(1, 1) + z_links(1, 1))
        unpack(1, 1)
        h_step(1, 2, deep)
        adjoint_last()

        part[...] = jnp.zeros_like(part)

        def seg(i):
            grad = COURANT * GR[i]
            coarse = grad.astype(jnp.bfloat16).astype(jnp.float32)
            fine = grad - coarse
            lhs = []
            for z in range(nz):
                hit = high_hot[i, :, z * ny:(z + 1) * ny] if stored else hits(i, z)
                cells = []
                for v in (coarse, fine):
                    line = jnp.broadcast_to(v[z:z + 1, :], (16, ny)).astype(jnp.bfloat16)
                    cells += [hit[q:q + 16] * line for q in range(0, n, 16)]
                lhs.append(jnp.concatenate(cells, axis=0))
            part[...] += lax.dot_general(
                jnp.concatenate(lhs, axis=1), low_hot[i],
                (((1,), (1,)), ((), ())), preferred_element_type=jnp.float32)

        each(0, nx, seg)

        total = part[0:n, :] + part[n:2 * n, :]
        total = jnp.concatenate([total, jnp.zeros((n, 128 - VOX_DEV), jnp.float32)], axis=1)
        for d in range(n):
            S[d] = total[d:d + 1, :]

        for s in range(3, len(stages)):
            pass_on(s)

        for dg in reversed(range(ng)):
            to_grp = (grp + dg) % ng

            def send_row(db, carry, to_grp=to_grp):
                to_blk = blk ^ (nb - 1 - db) if nb & (nb - 1) == 0 else (blk + nb - 1 - db) % nb
                pltpu.make_async_remote_copy(
                    S.at[to_grp * nb + to_blk], R.at[me], as_sem, ar_sem,
                    device_id=(to_grp, to_blk), device_id_type=MESH).start()
                return carry

            lax.fori_loop(0, nb if dg else nb - 1, send_row, 0, unroll=True)

        R[me] = S[me]
        rest = pl.ds(0, n - 1)
        pltpu.make_async_copy(R.at[rest], R.at[rest], ar_sem).wait()
        v_out[...] = jnp.sum(R[...], axis=0)[:, 0:VOX_DEV]
        pltpu.make_async_copy(S.at[rest], S.at[rest], as_sem).wait()
        for sends, copy in used:
            pl.when(sends)(copy.wait_send)

    return kernel


def write_out(e_in, h_in, v_in, e_out, h_out, v_out, sem):
    copies = [
        pltpu.make_async_copy(a, b, sem.at[j])
        for j, (a, b) in enumerate(((e_in, e_out), (h_in, h_out), (v_in, v_out)))
    ]
    for copy in copies:
        copy.start()
    for copy in copies:
        copy.wait()


def solution(mesh):
    ng, nb = mesh.shape["grp"], mesh.shape["blk"]
    n = ng * nb

    def local(e_field, h_field, inv_eps, cot_e, cot_h, voxel_ids):
        _, nx, nz, ny = e_field.shape
        f32 = jnp.float32
        plain = (3, nx, nz, ny)
        deep = (3, nx + 5, nz + 40, ny)
        dma = pltpu.SemaphoreType.DMA
        hbm = pl.BlockSpec(memory_space=pl.ANY)
        vmem = pl.BlockSpec(memory_space=pltpu.VMEM)
        e_new, h_new, vox = pl.pallas_call(
            make_kernel(ng, nb, nx, nz, ny),
            out_shape=(
                pltpu.VMEM(plain, f32),
                pltpu.VMEM(plain, f32),
                pltpu.VMEM((1, VOX_DEV), f32),
            ),
            in_specs=[hbm] * 6,
            out_specs=(vmem,) * 3,
            scratch_shapes=[
                pltpu.VMEM((2, STEPS) + deep, f32),
                pltpu.VMEM((2, STEPS + 1) + deep, f32),
                pltpu.VMEM(deep[1:], f32),
                pltpu.VMEM((2, 2, 4 * nz + 8, ny), f32),
                pltpu.VMEM((2, 2, 4 * nz + 8, ny), f32),
                pltpu.VMEM((2, 2, 4 * nz + 8, ny), f32),
                pltpu.VMEM((2, 2, 4 * nz + 8, ny), f32),
                pltpu.VMEM((2, 2, 12, nx, 1, ny), f32),
                pltpu.VMEM((2, 2, 12, nx, 1, ny), f32),
                pltpu.VMEM((2, 2, 9, nx, 1, ny), f32),
                pltpu.VMEM((2, 2, 9, nx, 1, ny), f32),
                pltpu.VMEM((2, 2, 4, 8, 1, ny), f32),
                pltpu.VMEM((2, 2, 4, 8, 1, ny), f32),
                pltpu.VMEM((3,) + plain, f32),
                pltpu.VMEM((2,) + plain, f32),
                pltpu.VMEM(plain[1:], f32),
                pltpu.VMEM(plain[1:], jnp.int32),
                pltpu.VMEM(plain[1:], f32),
                pltpu.VMEM((nx, VOX_DEV, nz * ny), jnp.bfloat16),
                pltpu.VMEM((nx, n if n <= STORED else 16, nz * ny), jnp.bfloat16),
                pltpu.VMEM((n, 1, 128), f32),
                pltpu.VMEM((n, 1, 128), f32),
                pltpu.VMEM((2 * n, VOX_DEV), f32),
                dma((7,)), dma, dma, dma((2, 2, 10)), dma((2, 2, 10)),
                pltpu.SemaphoreType.REGULAR((max(1, len(spread(nb))),)),
            ],
            compiler_params=pltpu.CompilerParams(
                collective_id=0, has_side_effects=True, vmem_limit_bytes=LIMIT),
        )(e_field, h_field, inv_eps, cot_e, cot_h, voxel_ids)
        e_new, h_new, vox = pl.pallas_call(
            write_out,
            out_shape=(
                jax.ShapeDtypeStruct(plain, f32),
                jax.ShapeDtypeStruct(plain, f32),
                jax.ShapeDtypeStruct((1, VOX_DEV), f32),
            ),
            in_specs=[hbm, hbm, hbm],
            out_specs=(hbm, hbm, hbm),
            scratch_shapes=[dma((3,))],
            compiler_params=pltpu.CompilerParams(vmem_limit_bytes=1024 * 1024),
        )(e_new, h_new, vox)
        return e_new, h_new, vox.reshape(VOX_DEV)

    field, cell = P(None, "blk", "grp", None), P("blk", "grp", None)
    return jax.shard_map(
        local, mesh=mesh,
        in_specs=(field, field, cell, field, field, cell),
        out_specs=(field, field, P(("grp", "blk"))),
        check_vma=False,
    )
```
